32 devices in a mesh: fsdp: 4 (over y, x), seq: 8 (over z, core).
Axes of the slice: x: 2, y: 2, z: 4, core: 2. Of those that a mesh axis runs over, the one named last changes fastest.
Arguments:
- block_input: float32 [4, 1024, 1024], P('fsdp', 'seq'), may hold values from -6 to 6
- norm_gain: float32 [1024], replicated, may hold values from 0.5 to 1.5
- w_in: bfloat16 [1024, 4384], P('fsdp', 'seq'), may hold values from -0.1875 to 0.1875
- conv_w: float32 [4, 2304], replicated, may hold values from -0.5 to 0.5
- conv_b: float32 [2304], replicated, may hold values from -0.5 to 0.5
- dt_bias: float32 [32], replicated, may hold values from -6.5 to -2.5
- a_log: float32 [32], replicated, may hold values from 0 to 2.77
- skip_gain: float32 [32], replicated, may hold values from 0.5 to 1.5
- gate_gain: float32 [2048], replicated, may hold values from 0.5 to 1.5
- w_out: bfloat16 [2048, 1024], P('fsdp', 'seq'), may hold values from -0.125 to 0.125
- out_cotangent: float32 [4, 1024, 1024], P('fsdp', 'seq'), may hold values from -6 to 6
Outputs:
- block_output: float32 [4, 1024, 1024], P('fsdp', 'seq')
- grad_input: float32 [4, 1024, 1024], P('fsdp', 'seq')
- grad_norm_gain: float32 [1024], replicated
- grad_w_in: float32 [1024, 4384], P('fsdp', 'seq')
- grad_conv_w: float32 [4, 2304], replicated
- grad_conv_b: float32 [2304], replicated
- grad_dt_bias: float32 [32], replicated
- grad_a_log: float32 [32], replicated
- grad_skip_gain: float32 [32], replicated
- grad_gate_gain: float32 [2048], replicated
- grad_w_out: float32 [2048, 1024], P('fsdp', 'seq')
The draws below stay inside these ranges and needn't reach their ends.
All inputs are finite; a program needn't handle non-finite values.
Results may differ from the reference program's by a relative error of at most 0.011.
Values may be sent and summed in bfloat16 or wider, within the bound.
No kernel may reach another device: no remote copies, remote signals or barrier semaphores. Data moves between devices by JAX's collectives and lax.ppermute only.
A program may use at most 128 MiB of HBM per device.

```python
import jax
import jax.numpy as jnp
from jax import lax

D = 1024
DI = 2048
HEADS = 32
HEAD_DIM = 64
STATE = 128
CONV_W = 4
GROUP = 128
LEN = 1024
SEQS = 4
PROJ = 4384
CONV_CH = 2304


def steps_of(own_key, shape, split, smallest, top_value):
    factor_of, own = 1.0, jax.random.fold_in(own_key, 6)
    for dim, shards_of in split:
        heights = jnp.exp(jax.random.uniform(jax.random.fold_in(own, dim), (shards_of,), jnp.float32, smallest / len(split), top_value / len(split)))
        factor_of = factor_of * jnp.repeat(heights, shape[dim] // shards_of).reshape([-1 if axis == dim else 1 for axis in range(len(shape))])
    return factor_of


def gaussian(own_key, shape, width, most, shards=(), kind=jnp.bfloat16):
    factor_of = steps_of(own_key, shape, shards, -0.22, 0.18) if shards else 1.0
    values = jax.random.normal(own_key, shape, jnp.float32) * width * factor_of
    return jnp.minimum(jnp.maximum(values, -most), most).astype(kind)


def setup_inputs(seed: int = 0) -> dict:
    arg_keys = jax.random.split(jax.random.key(seed), 12)
    return {
        "block_input": gaussian(arg_keys[0], (SEQS, LEN, D), 1.0, 6.0, ((0, 4), (1, 8)), jnp.float32),
        "norm_gain": jnp.clip(1.0 + 0.1 * jax.random.normal(arg_keys[1], (D,), jnp.float32), 0.5, 1.5),
        "w_in": gaussian(arg_keys[2], (D, PROJ), D ** -0.5, 0.1875, ((0, 4), (1, 8))),
        "conv_w": jnp.clip(jax.random.uniform(arg_keys[3], (CONV_W, CONV_CH), jnp.float32, -0.5, 0.5), -0.5, 0.5),
        "conv_b": jnp.clip(jax.random.uniform(arg_keys[4], (CONV_CH,), jnp.float32, -0.5, 0.5), -0.5, 0.5),
        "dt_bias": jnp.clip(jax.random.uniform(arg_keys[5], (HEADS,), jnp.float32, -6.5, -2.5), -6.5, -2.5),
        "a_log": jnp.clip(jax.random.uniform(arg_keys[6], (HEADS,), jnp.float32, 0.0, 2.77), 0.0, 2.77),
        "skip_gain": jnp.clip(jax.random.uniform(arg_keys[7], (HEADS,), jnp.float32, 0.5, 1.5), 0.5, 1.5),
        "gate_gain": jnp.clip(1.0 + 0.1 * jax.random.normal(arg_keys[8], (DI,), jnp.float32), 0.5, 1.5),
        "w_out": gaussian(arg_keys[9], (DI, D), DI ** -0.5, 0.125, ((0, 4), (1, 8))),
        "out_cotangent": gaussian(arg_keys[10], (SEQS, LEN, D), 1.0, 6.0, ((0, 4), (1, 8)), jnp.float32),
    }


EPS = 1e-05

def rms_apply(values, norm_gain):
    return values * lax.rsqrt(lax.optimization_barrier(jnp.mean(values * values, axis=-1, keepdims=True)) + EPS) * norm_gain

def gated_apply(values, gate_values, norm_gain):
    return rms_apply(values * jax.nn.silu(gate_values), norm_gain)

def causal_conv(signal, kernel, offset):
    taps = kernel.shape[0]
    length = signal.shape[0]
    padded = jnp.pad(signal, ((taps - 1, 0), (0, 0)))
    summed = offset + kernel[0] * padded[0:length]
    for tap_index in range(1, taps):
        summed = summed + kernel[tap_index] * padded[tap_index:tap_index + length]
    return jax.nn.silu(summed)

def state_space(signal, step_size, b_rows, c_rows, log_rate, skip_value):
    length = signal.shape[0]
    channels = signal.shape[1]
    blocks = length // GROUP
    highest = lax.Precision.HIGHEST
    decay_rate = -jnp.exp(log_rate) * step_size
    x_blocks = signal.reshape(blocks, GROUP, channels)
    step_blocks = step_size.reshape(blocks, GROUP)
    b_blocks = b_rows.reshape(blocks, GROUP, b_rows.shape[1])
    c_blocks = c_rows.reshape(blocks, GROUP, c_rows.shape[1])
    running = jnp.cumsum(decay_rate.reshape(blocks, GROUP), axis=1)
    scores = jnp.einsum('cin,cjn->cij', c_blocks, b_blocks, precision=highest)
    row_index = lax.broadcasted_iota(jnp.int32, (GROUP, GROUP), 0)
    col_index = lax.broadcasted_iota(jnp.int32, (GROUP, GROUP), 1)
    causal = row_index >= col_index
    spread = running[:, :, None] - running[:, None, :]
    decay = jnp.where(causal, jnp.exp(jnp.where(causal, spread, 0.0)), 0.0)
    within = jnp.einsum('cij,cjp->cip', scores * decay * step_blocks[:, None, :], x_blocks, precision=highest)
    toward = jnp.exp(running[:, -1:] - running) * step_blocks
    inflow = jnp.einsum('cjp,cjn->cpn', x_blocks * toward[:, :, None], b_blocks, precision=highest)
    carried = jnp.exp(running[:, -1])

    def advance(memory, packet):
        factor, update = packet
        return (factor * memory + update, memory)
    _, openings = lax.scan(advance, jnp.zeros((channels, b_rows.shape[1]), signal.dtype), (carried, inflow))
    across = jnp.exp(running)[:, :, None] * jnp.einsum('cin,cpn->cip', c_blocks, openings, precision=highest)
    return (within + across).reshape(length, channels) + skip_value * signal

def mixer_head(x_raw, dt_raw, b_raw, c_raw, kern_x, bias_x, kern_b, bias_b, kern_c, bias_c, log_rate, skip_value, dt_shift):
    x_act = causal_conv(x_raw, kern_x, bias_x)
    b_act = causal_conv(b_raw, kern_b, bias_b)
    c_act = causal_conv(c_raw, kern_c, bias_c)
    step_size = jax.nn.softplus(dt_raw + dt_shift)
    return state_space(x_act, step_size, b_act, c_act, log_rate, skip_value)

def reference(block_input, norm_gain, w_in, conv_w, conv_b, dt_bias, a_log, skip_gain, gate_gain, w_out, out_cotangent):
    kern_x = conv_w[:, :DI].reshape(CONV_W, HEADS, HEAD_DIM).transpose(1, 0, 2)
    bias_x = conv_b[:DI].reshape(HEADS, HEAD_DIM)
    kern_b = conv_w[:, DI:DI + STATE]
    kern_c = conv_w[:, DI + STATE:]
    bias_b = conv_b[DI:DI + STATE]
    bias_c = conv_b[DI + STATE:]

    def one_sequence(totals, packet):
        residual, grad_out = packet
        normed, norm_pull = jax.vjp(rms_apply, residual, norm_gain)
        normed_half = normed.astype(jnp.bfloat16)
        projected = jnp.dot(normed_half, w_in, preferred_element_type=jnp.float32).astype(jnp.bfloat16)
        gate_half = projected[:, :DI]
        x_raw = projected[:, DI:2 * DI].astype(jnp.float32).reshape(LEN, HEADS, HEAD_DIM).transpose(1, 0, 2)
        b_raw = projected[:, 2 * DI:2 * DI + STATE].astype(jnp.float32)
        c_raw = projected[:, 2 * DI + STATE:2 * DI + 2 * STATE].astype(jnp.float32)
        dt_raw = projected[:, 2 * DI + 2 * STATE:].astype(jnp.float32).T

        def head_forward(packet_h):
            xr_h, dr_h, kx_h, bx_h, lr_h, sk_h, sh_h = packet_h
            return mixer_head(xr_h, dr_h, b_raw, c_raw, kx_h, bx_h, kern_b, bias_b, kern_c, bias_c, lr_h, sk_h, sh_h).astype(jnp.bfloat16)
        y_half = lax.map(head_forward, (x_raw, dt_raw, kern_x, bias_x, a_log, skip_gain, dt_bias))
        y_tokens = y_half.transpose(1, 0, 2).reshape(LEN, DI)
        gated, gate_pull = jax.vjp(gated_apply, y_tokens.astype(jnp.float32), gate_half.astype(jnp.float32), gate_gain)
        gated_half = gated.astype(jnp.bfloat16)
        block_out = residual + jnp.dot(gated_half, w_out, preferred_element_type=jnp.float32)
        cot_half = grad_out.astype(jnp.bfloat16)
        g_w_out = jnp.dot(gated_half.T, cot_half, preferred_element_type=jnp.float32)
        dgated = jnp.dot(cot_half, w_out.T, preferred_element_type=jnp.float32)
        grad_y, grad_z, g_gate = gate_pull(dgated)
        dy_heads = grad_y.astype(jnp.bfloat16).reshape(LEN, HEADS, HEAD_DIM).transpose(1, 0, 2)

        def head_backward(packet_h):
            xr_h, dr_h, kx_h, bx_h, lr_h, sk_h, sh_h, cot_h = packet_h
            _, pull_h = jax.vjp(mixer_head, xr_h, dr_h, b_raw, c_raw, kx_h, bx_h, kern_b, bias_b, kern_c, bias_c, lr_h, sk_h, sh_h)
            return pull_h(cot_h.astype(jnp.float32))
        pieces = lax.map(head_backward, (x_raw, dt_raw, kern_x, bias_x, a_log, skip_gain, dt_bias, dy_heads))
        g_xr, g_dtr, g_br, g_cr, g_kx, g_bx, g_kb, g_bb, g_kc, g_bc, g_rate, g_skip, g_shift = pieces
        dx_tokens = g_xr.astype(jnp.bfloat16).transpose(1, 0, 2).reshape(LEN, DI)
        ddt_tokens = g_dtr.astype(jnp.bfloat16).T
        db_tokens = lax.optimization_barrier(jnp.sum(g_br, axis=0)).astype(jnp.bfloat16)
        dc_tokens = lax.optimization_barrier(jnp.sum(g_cr, axis=0)).astype(jnp.bfloat16)
        dproj = jnp.concatenate([grad_z.astype(jnp.bfloat16), dx_tokens, db_tokens, dc_tokens, ddt_tokens], axis=1)
        g_w_in = jnp.dot(normed_half.T, dproj, preferred_element_type=jnp.float32)
        dnormed = jnp.dot(dproj, w_in.T, preferred_element_type=jnp.float32)
        du_norm, g_norm = norm_pull(dnormed)
        grad_in = grad_out + du_norm
        g_conv_w = jnp.concatenate([g_kx.transpose(1, 0, 2).reshape(CONV_W, DI), lax.optimization_barrier(jnp.sum(g_kb, axis=0)), lax.optimization_barrier(jnp.sum(g_kc, axis=0))], axis=1)
        g_conv_b = jnp.concatenate([g_bx.reshape(DI), lax.optimization_barrier(jnp.sum(g_bb, axis=0)), lax.optimization_barrier(jnp.sum(g_bc, axis=0))])
        fresh = (g_norm, g_w_in, g_conv_w, g_conv_b, g_shift, g_rate, g_skip, g_gate, g_w_out)
        updated = tuple((older + newer for older, newer in zip(totals, fresh)))
        return (updated, (block_out, grad_in))
    initial = (jnp.zeros((D,), jnp.float32), jnp.zeros((D, PROJ), jnp.float32), jnp.zeros((CONV_W, CONV_CH), jnp.float32), jnp.zeros((CONV_CH,), jnp.float32), jnp.zeros((HEADS,), jnp.float32), jnp.zeros((HEADS,), jnp.float32), jnp.zeros((HEADS,), jnp.float32), jnp.zeros((DI,), jnp.float32), jnp.zeros((DI, D), jnp.float32))
    totals, (outputs, grads_in) = lax.scan(one_sequence, initial, (block_input, out_cotangent))
    return (outputs, grads_in, totals[0], totals[1], totals[2], totals[3], totals[4], totals[5], totals[6], totals[7], totals[8])
```

```python
import functools

import jax
import jax.numpy as jnp
import numpy as np
from jax import lax
from jax.experimental import pallas as pl
from jax.experimental.pallas import tpu as pltpu
from jax.sharding import PartitionSpec as P

HEAD_DIM = 64
STATE = 128
CONV_W = 4
GROUP = 128
LANES = 128
EPS = 1e-05
HALO = 8
BF = jnp.bfloat16
F32 = jnp.float32
HIGH = lax.Precision.HIGHEST


def ceil_to(n, k):
    return (n + k - 1) // k * k


def dot(a, b, ca, cb, precision=None):
    return lax.dot_general(
        a, b, (((ca,), (cb,)), ((), ())), precision=precision, preferred_element_type=F32
    )


class Routes:
    def __init__(self, seq, columns, inner, state, heads):
        self.seq = seq
        self.pair = 2 if seq % 2 == 0 else 1
        self.own = columns // seq
        self.width = inner // seq
        self.shared = 2 * state + heads
        self.heads_here = heads // seq
        width, own, pair = self.width, self.own, self.pair
        pieces = []
        for dst in range(seq):
            wants = [(dst * width, width, 0), (inner + dst * width, width, width)]
            if dst % pair == pair - 1:
                wants.append((2 * inner, self.shared, 2 * width))
            for start, length, at in wants:
                col = start
                while col < start + length:
                    src = col // own
                    stop = min(start + length, (src + 1) * own)
                    pieces.append((src, dst, col - src * own, stop - col, at + col - start))
                    col = stop
        self.local = [p for p in pieces if p[0] == p[1]]
        remote = [p for p in pieces if p[0] != p[1]]
        self.rounds = self.color(remote)
        self.length = ceil_to(max([p[3] for p in remote] + [1]), 16)
        n, m = len(self.rounds), self.length
        self.rows = 2 * width + self.shared
        self.send = np.full((seq, n * m), -1, np.int32)
        self.take = np.full((seq, self.rows), -1, np.int32)
        self.back = np.full((seq, n * m), -1, np.int32)
        self.home = np.full((seq, self.rows + n * m), -1, np.int32)
        for src, dst, at, length, to in self.local:
            for i in range(length):
                self.take[dst, to + i] = at + i
                self.home[dst, to + i] = at + i
        for r, group in enumerate(self.rounds):
            for src, dst, at, length, to in group:
                for i in range(length):
                    self.send[src, r * m + i] = at + i
                    self.take[dst, to + i] = own + r * m + i
                    self.back[dst, r * m + i] = to + i
                    self.home[src, self.rows + r * m + i] = at + i

    @staticmethod
    def color(pieces):
        rounds = []
        left = sorted(pieces, key=lambda p: -p[3])
        degree = {}
        for p in left:
            degree[("s", p[0])] = degree.get(("s", p[0]), 0) + 1
            degree[("d", p[1])] = degree.get(("d", p[1]), 0) + 1
        limit = max(degree.values()) if degree else 0
        used = {}
        colors = {}

        def free(node):
            taken = used.setdefault(node, {})
            return next(c for c in range(limit) if c not in taken)

        for index, p in enumerate(left):
            u, v = ("s", p[0]), ("d", p[1])
            a, b = free(u), free(v)
            if a != b and a in used[v]:
                path, node, want = [], v, a
                while want in used[node]:
                    edge = used[node][want]
                    path.append(edge)
                    q = left[edge]
                    ends = (("s", q[0]), ("d", q[1]))
                    node = ends[1] if node == ends[0] else ends[0]
                    want = b if want == a else a
                for edge in path:
                    q = left[edge]
                    for end in (("s", q[0]), ("d", q[1])):
                        used[end].pop(colors[edge], None)
                for edge in path:
                    q = left[edge]
                    colors[edge] = b if colors[edge] == a else a
                    for end in (("s", q[0]), ("d", q[1])):
                        used[end][colors[edge]] = edge
            colors[index] = a
            used[u][a] = index
            used[v][a] = index
        for c in range(limit):
            rounds.append([left[i] for i in range(len(left)) if colors[i] == c])
        return rounds


def one_hot(index, size):
    return (index[:, None] == lax.broadcasted_iota(jnp.int32, (index.shape[0], size), 1)).astype(BF)


def row_of(table, at):
    return lax.dynamic_index_in_dim(jnp.asarray(table), at, 0, keepdims=False)


class Links:
    def __init__(self, fsdp, seq):
        self.F, self.S = fsdp, seq
        self.pair = 2 if seq % 2 == 0 else 1
        self.chips = seq // self.pair
        self.f = lax.axis_index("fsdp")
        self.s = lax.axis_index("seq")
        self.chip = self.s // self.pair
        self.core = self.s % self.pair

    def swap(self, x):
        return lax.ppermute(x, "seq", [(i, i ^ 1) for i in range(self.S)])

    def hop(self, x, k):
        step = self.pair * k
        return lax.ppermute(x, "seq", [(i, (i + step) % self.S) for i in range(self.S)])

    def chip_at(self, k):
        return lax.rem(self.chip + k + self.chips, self.chips)

    def across(self, x, k):
        if self.F & (self.F - 1) == 0:
            pairs = [(i, i ^ k) for i in range(self.F)]
        else:
            pairs = [(i, (i + k) % self.F) for i in range(self.F)]
        return lax.ppermute(x, "fsdp", pairs)

    def peer_to(self, k):
        return self.f ^ k if self.F & (self.F - 1) == 0 else lax.rem(self.f + k, self.F)

    def peer_from(self, k):
        return self.f ^ k if self.F & (self.F - 1) == 0 else lax.rem(self.f - k + self.F, self.F)

    def interleave(self, mine, other):
        if self.pair == 1:
            return mine[:, None]
        first = self.core == 0
        return jnp.stack([jnp.where(first, mine, other), jnp.where(first, other, mine)], 1)

    def gather_seq(self, x):
        mine = jnp.zeros((self.chips,) + x.shape, x.dtype)
        mine = lax.dynamic_update_index_in_dim(mine, x, self.chip, 0)
        for k in range(1, self.chips):
            mine = lax.dynamic_update_index_in_dim(mine, self.hop(x, k), self.chip_at(-k), 0)
        if self.pair == 1:
            return mine
        both = self.interleave(mine, self.swap(mine))
        return both.reshape((self.S,) + x.shape)

    def scatter_seq(self, parts):
        shape = parts.shape[1:]
        parts = parts.reshape((self.chips, self.pair) + shape)
        if self.pair == 2:
            keep = lax.dynamic_index_in_dim(parts, self.core, 1, keepdims=False)
            give = lax.dynamic_index_in_dim(parts, 1 - self.core, 1, keepdims=False)
            held = (keep.astype(F32) + self.swap(give).astype(F32)).astype(BF)
        else:
            held = parts[:, 0]
        total = lax.dynamic_index_in_dim(held, self.chip, 0, keepdims=False).astype(F32)
        for k in range(1, self.chips):
            piece = lax.dynamic_index_in_dim(held, self.chip_at(k), 0, keepdims=False)
            total = total + self.hop(piece, k).astype(F32)
        return total

    def exchange_seq(self, parts):
        shape = parts.shape[1:]
        parts = parts.reshape((self.chips, self.pair) + shape)
        got = jnp.zeros_like(parts)
        own = lax.dynamic_index_in_dim(parts, self.chip, 0, keepdims=False)
        got = lax.dynamic_update_index_in_dim(got, own, self.chip, 0)
        for k in range(1, self.chips):
            piece = lax.dynamic_index_in_dim(parts, self.chip_at(k), 0, keepdims=False)
            got = lax.dynamic_update_index_in_dim(got, self.hop(piece, k), self.chip_at(-k), 0)
        if self.pair == 1:
            return got.reshape((self.S,) + shape)
        mine = lax.dynamic_index_in_dim(got, self.core, 1, keepdims=False)
        give = lax.dynamic_index_in_dim(got, 1 - self.core, 1, keepdims=False)
        return self.interleave(mine, self.swap(give)).reshape((self.S,) + shape)

    def gather_fsdp(self, x):
        out = jnp.zeros((self.F,) + x.shape, x.dtype)
        out = lax.dynamic_update_index_in_dim(out, x, self.f, 0)
        for k in range(1, self.F):
            out = lax.dynamic_update_index_in_dim(out, self.across(x, k), self.peer_from(k), 0)
        return out

    def scatter_fsdp(self, parts):
        total = lax.dynamic_index_in_dim(parts, self.f, 0, keepdims=False).astype(F32)
        for k in range(1, self.F):
            piece = lax.dynamic_index_in_dim(parts, self.peer_to(k), 0, keepdims=False)
            total = total + self.across(piece, k).astype(F32)
        return total

    def sum_axis(self, x, axis):
        size = self.S if axis == "seq" else self.F
        if size & (size - 1):
            return lax.psum(x, axis)
        k = 1
        while k < size:
            x = x + lax.ppermute(x, axis, [(i, i ^ k) for i in range(size)])
            k *= 2
        return x


def spread(values, heads):
    rows = values.shape[0]
    return jnp.concatenate(
        [jnp.broadcast_to(values[:, h : h + 1], (rows, HEAD_DIM)) for h in range(heads)], axis=1
    )


def softplus(x):
    return jnp.maximum(x, 0.0) + jnp.log1p(jnp.exp(-jnp.abs(x)))


def tri(lower):
    row = lax.broadcasted_iota(jnp.int32, (GROUP, GROUP), 0)
    col = lax.broadcasted_iota(jnp.int32, (GROUP, GROUP), 1)
    return (row >= col) if lower else (row <= col)


def conv_taps(v, halo):
    ext = jnp.concatenate([halo, v], axis=0)
    return [
        (pltpu.roll(ext, CONV_W - 1 - k, 0) if k < CONV_W - 1 else ext)[HALO:]
        for k in range(CONV_W)
    ]


def conv_pre(taps, cw, cb):
    pre = cb + cw[0:1] * taps[0]
    for k in range(1, CONV_W):
        pre = pre + cw[k : k + 1] * taps[k]
    return pre


def halo_of(proj_ref, i, lo, hi):
    start = pl.multiple_of(jnp.maximum(i * GROUP - 16, 0), 16)
    rows = proj_ref[pl.ds(start, 16), lo:hi].astype(F32)[16 - HALO :]
    return jnp.where(i > 0, rows, 0.0)


def forward_kernel(
    heads, normed_ref, w_ref, cw_ref, cb_ref, hp_ref, proj_ref, y_ref, core_ref, open_ref, state
):
    width = heads * HEAD_DIM
    chans = width + 2 * STATE
    state[...] = jnp.zeros_like(state)
    shards, _, depth = w_ref.shape

    def step(i, _):
        rows = pl.ds(pl.multiple_of(i * GROUP, GROUP), GROUP)
        acc = dot(normed_ref[rows, 0:depth], w_ref[0], 1, 1)
        for f in range(1, shards):
            acc = acc + dot(normed_ref[rows, f * depth : (f + 1) * depth], w_ref[f], 1, 1)
        proj = acc.astype(BF)
        proj_ref[rows, :] = proj
        v = proj[:, width : width + chans].astype(F32)
        taps = conv_taps(v, halo_of(proj_ref, i, width, width + chans))
        pre = conv_pre(taps, cw_ref[...], cb_ref[...])
        act = pre * jax.nn.sigmoid(pre)
        xs = act[:, :width]
        bs = act[:, width : width + STATE].astype(BF)
        cs = act[:, width + STATE :].astype(BF)
        dt = softplus(proj[:, width + chans :].astype(F32) + hp_ref[0:1])
        rate = -jnp.exp(hp_ref[1:2]) * dt
        run = dot(tri(True).astype(F32), rate, 1, 0, HIGH)
        run_t = run.T
        last = run[GROUP - 1 : GROUP]
        xdt = (xs * spread(dt, heads)).astype(BF)
        scores = dot(cs, bs, 1, 1)
        causal = tri(True)
        within = []
        for h in range(heads):
            gap = run[:, h : h + 1] - run_t[h : h + 1, :]
            decay = jnp.exp(jnp.where(causal, gap, -1e30))
            mixed = (scores * decay).astype(BF)
            within.append(dot(mixed, xdt[:, h * HEAD_DIM : (h + 1) * HEAD_DIM], 1, 0))
        memory = state[...]
        open_ref[i] = memory
        core = jnp.concatenate(within, axis=1) + spread(jnp.exp(run), heads) * dot(
            cs, memory.astype(BF), 1, 0
        )
        core_ref[rows, :] = core
        y_ref[rows, :] = (core + spread(hp_ref[2:3], heads) * xs).astype(BF)
        toward = (xdt.astype(F32) * spread(jnp.exp(last - run), heads)).astype(BF)
        state[...] = spread(jnp.exp(last), heads) * memory + dot(bs, toward, 0, 0)
        return 0

    lax.fori_loop(0, normed_ref.shape[0] // GROUP, step, 0)


def stats_kernel(cot_ref, wo_ref, y_ref, proj_ref, gain_ref, dg_ref, stats_ref):
    width = y_ref.shape[1]
    ones = jnp.ones((8, width), F32)

    def step(i, _):
        rows = pl.ds(pl.multiple_of(i * GROUP, GROUP), GROUP)
        dg = dot(cot_ref[rows, :], wo_ref[...], 1, 1)
        dg_ref[rows, :] = dg
        z = proj_ref[rows, :width].astype(F32)
        u = y_ref[rows, :].astype(F32) * (z * jax.nn.sigmoid(z))
        stats_ref[0:1, rows] = dot(ones, u * u, 1, 1, HIGH)[0:1]
        stats_ref[1:2, rows] = dot(ones, u * gain_ref[...] * dg, 1, 1, HIGH)[0:1]
        return 0

    lax.fori_loop(0, cot_ref.shape[0] // GROUP, step, 0)


def gate_kernel(
    inner,
    cot_ref,
    wo_ref,
    y_ref,
    proj_ref,
    gain_ref,
    dg_ref,
    stats_ref,
    out_ref,
    gwo_ref,
    dy_ref,
    dz_ref,
    ggain_ref,
    acc,
):
    width = y_ref.shape[1]
    acc[...] = jnp.zeros_like(acc)
    ggain_ref[...] = jnp.zeros_like(ggain_ref)
    gain = gain_ref[...]

    def step(i, _):
        rows = pl.ds(pl.multiple_of(i * GROUP, GROUP), GROUP)
        st = jnp.concatenate([stats_ref[:, rows], jnp.zeros((6, GROUP), F32)], axis=0).T
        r = lax.rsqrt(st[:, 0:1] / inner + EPS)
        y = y_ref[rows, :].astype(F32)
        z = proj_ref[rows, :width].astype(F32)
        sig = jax.nn.sigmoid(z)
        sz = z * sig
        u = y * sz
        dg = dg_ref[rows, :]
        ur = u * r
        gated = (ur * gain).astype(BF)
        du = r * (gain * dg) - u * (r * r * r * (st[:, 1:2] / inner))
        ggain_ref[...] += jnp.sum(dg * ur, axis=0, keepdims=True)
        dy_ref[rows, :] = (du * sz).astype(BF)
        dz_ref[rows, :] = (du * y * (sig * (1.0 + z * (1.0 - sig)))).astype(BF)
        out_ref[rows, :] = dot(gated, wo_ref[...], 1, 0).astype(BF)
        acc[...] += dot(gated, cot_ref[rows, :], 0, 0)
        return 0

    lax.fori_loop(0, cot_ref.shape[0] // GROUP, step, 0)
    gwo_ref[...] = acc[...].astype(BF)


def backward_kernel(
    heads,
    proj_ref,
    core_ref,
    open_ref,
    dy_ref,
    dz_ref,
    cw_ref,
    cb_ref,
    hp_ref,
    dproj_ref,
    gcw_ref,
    gcb_ref,
    ghp_ref,
    dstate,
    ahead,
):
    width = heads * HEAD_DIM
    chans = width + 2 * STATE
    blocks = proj_ref.shape[0] // GROUP
    dstate[...] = jnp.zeros_like(dstate)
    ahead[...] = jnp.zeros_like(ahead)
    gcw_ref[...] = jnp.zeros_like(gcw_ref)
    gcb_ref[...] = jnp.zeros_like(gcb_ref)
    ghp_ref[...] = jnp.zeros_like(ghp_ref)
    fold = (
        lax.broadcasted_iota(jnp.int32, (width, LANES), 0) // HEAD_DIM
        == lax.broadcasted_iota(jnp.int32, (width, LANES), 1)
    ).astype(F32)

    def step(n, _):
        i = blocks - 1 - n
        rows = pl.ds(pl.multiple_of(i * GROUP, GROUP), GROUP)
        v = proj_ref[rows, width : width + chans].astype(F32)
        taps = conv_taps(v, halo_of(proj_ref, i, width, width + chans))
        cw = cw_ref[...]
        pre = conv_pre(taps, cw, cb_ref[...])
        sig = jax.nn.sigmoid(pre)
        act = pre * sig
        xs = act[:, :width]
        bs = act[:, width : width + STATE].astype(BF)
        cs = act[:, width + STATE :].astype(BF)
        shifted = proj_ref[rows, width + chans :].astype(F32) + hp_ref[0:1]
        dt = softplus(shifted)
        neg = -jnp.exp(hp_ref[1:2])
        rate = neg * dt
        run = dot(tri(True).astype(F32), rate, 1, 0, HIGH)
        run_t = run.T
        last = run[GROUP - 1 : GROUP]
        dt_x = spread(dt, heads)
        xdt = (xs * dt_x).astype(BF)
        scores = dot(cs, bs, 1, 1)
        causal = tri(True)
        dyb = dy_ref[rows, :]
        dy = dyb.astype(F32)
        dscores = jnp.zeros((GROUP, GROUP), F32)
        parts = []
        for h in range(heads):
            cols = slice(h * HEAD_DIM, (h + 1) * HEAD_DIM)
            gap = run[:, h : h + 1] - run_t[h : h + 1, :]
            decay = jnp.exp(jnp.where(causal, gap, -1e30))
            mixed = (scores * decay).astype(BF)
            parts.append(dot(mixed, dyb[:, cols], 0, 0))
            dscores = dscores + dot(dyb[:, cols], xdt[:, cols], 1, 1) * decay
        dscores = dscores.astype(BF)
        memory = open_ref[i]
        mem_b = memory.astype(BF)
        ds = dstate[...]
        ds_b = ds.astype(BF)
        edy = (spread(jnp.exp(run), heads) * dy).astype(BF)
        dec = spread(jnp.exp(last - run), heads)
        xdt_f = xdt.astype(F32)
        inflow = dec * dot(bs, ds_b, 1, 0)
        dxdt = jnp.concatenate(parts, axis=1) + inflow
        dc = dot(dscores, bs, 1, 0) + dot(edy, mem_b, 1, 1)
        db = dot(dscores, cs, 0, 0) + dot((xdt_f * dec).astype(BF), ds_b, 1, 1)
        carried = spread(jnp.exp(last), heads)
        dstate[...] = dot(cs, edy, 0, 0) + carried * ds
        dx = dt_x * dxdt + spread(hp_ref[2:3], heads) * dy
        tops = jnp.concatenate(
            [
                jnp.sum(xdt_f * inflow, axis=0, keepdims=True)
                + carried * jnp.sum(ds * memory, axis=0, keepdims=True),
                jnp.sum(dy * xs, axis=0, keepdims=True),
                jnp.zeros((6, width), F32),
            ],
            axis=0,
        )
        folded = dot(
            jnp.concatenate([xs * dxdt, dy * core_ref[rows, :] - xdt_f * dxdt, tops], axis=0),
            fold,
            1,
            0,
            HIGH,
        )
        dend = folded[2 * GROUP : 2 * GROUP + 1]
        drate = dot(tri(False).astype(F32), folded[GROUP : 2 * GROUP], 1, 0, HIGH) + dend
        ddt = folded[:GROUP] + neg * drate
        ddtr = ddt * jax.nn.sigmoid(shifted)
        ghp_ref[0:1] += jnp.sum(ddtr, axis=0, keepdims=True)
        ghp_ref[1:2] += jnp.sum(drate * rate, axis=0, keepdims=True)
        ghp_ref[2:3] += folded[2 * GROUP + 1 : 2 * GROUP + 2]
        dact = jnp.concatenate([dx, db, dc], axis=1)
        dpre = dact * (sig * (1.0 + pre * (1.0 - sig)))
        gcb_ref[...] += jnp.sum(dpre, axis=0, keepdims=True)
        for k in range(CONV_W):
            gcw_ref[k : k + 1] += jnp.sum(dpre * taps[k], axis=0, keepdims=True)
        ext = jnp.concatenate([dpre, ahead[...]], axis=0)
        ahead[...] = dpre[:HALO]
        dv = cw[CONV_W - 1 :] * dpre
        for k in range(CONV_W - 1):
            moved = pltpu.roll(ext, ext.shape[0] - (CONV_W - 1 - k), 0)[:GROUP]
            dv = dv + cw[k : k + 1] * moved
        dproj_ref[rows, :width] = dz_ref[rows, :]
        dproj_ref[rows, width : width + chans] = dv.astype(BF)
        dproj_ref[rows, width + chans :] = ddtr.astype(BF)
        return 0

    lax.fori_loop(0, blocks, step, 0)


def call(kernel, outs, scratch, *args):
    whole = pl.BlockSpec(memory_space=pltpu.VMEM)
    return pl.pallas_call(
        kernel,
        out_shape=[jax.ShapeDtypeStruct(shape, kind) for shape, kind in outs],
        in_specs=[whole] * len(args),
        out_specs=[whole] * len(outs),
        scratch_shapes=[pltpu.VMEM(shape, kind) for shape, kind in scratch],
    )(*args)


def per_device(
    fsdp,
    seq,
    block_input,
    norm_gain,
    w_in,
    conv_w,
    conv_b,
    dt_bias,
    a_log,
    skip_gain,
    gate_gain,
    w_out,
    out_cotangent,
):
    links = Links(fsdp, seq)
    residual = block_input[0]
    grad_out = out_cotangent[0]
    tokens, depth = residual.shape
    length = tokens * seq
    heads_all = dt_bias.shape[0]
    inner = gate_gain.shape[0]
    heads = heads_all // seq
    width = inner // seq
    chans = width + 2 * STATE
    routes = Routes(seq, w_in.shape[1] * seq, inner, STATE, heads_all)
    me, rounds, msg = links.s, len(routes.rounds), routes.length
    shared = routes.shared

    mean = jnp.mean(residual * residual, axis=-1, keepdims=True)
    scale = lax.rsqrt(mean + EPS)
    normed_half = (residual * scale * norm_gain).astype(BF)

    picked = dot(one_hot(row_of(routes.send, me), w_in.shape[1]), w_in, 1, 1).astype(BF)
    arrived = [dot_rows(w_in)]
    for r, group in enumerate(routes.rounds):
        arrived.append(
            lax.ppermute(picked[r * msg : (r + 1) * msg], "seq", [(p[0], p[1]) for p in group])
        )
    pool = jnp.concatenate(arrived, axis=0)
    mine = dot(one_hot(row_of(routes.take, me), pool.shape[0]), pool, 1, 0).astype(BF)
    common = mine[2 * width :]
    if links.pair == 2:
        common = common + lax.ppermute(
            common, "seq", [(i, i - 1) for i in range(1, seq, 2)]
        )
    head_row = jnp.arange(LANES, dtype=jnp.int32)
    head_row = jnp.where(head_row < heads, 2 * STATE + me * heads + head_row, -1)
    head_pick = one_hot(head_row, shared)
    w_mine = jnp.concatenate(
        [mine[: 2 * width], common[: 2 * STATE], dot(head_pick, common, 1, 0).astype(BF)], axis=0
    )
    normed_all = links.gather_seq(normed_half).reshape(length, depth)
    w_all = links.gather_fsdp(w_mine)

    wo_rows = links.gather_fsdp(w_out).reshape(seq, width, w_out.shape[1])
    wo = links.exchange_seq(wo_rows).transpose(1, 0, 2).reshape(width, depth)
    cot_half = grad_out.astype(BF)
    cot_half, _ = lax.optimization_barrier((cot_half, normed_all))
    cot_all = links.gather_seq(cot_half).reshape(length, depth)

    def local(vector, size, start):
        return lax.dynamic_slice_in_dim(vector, start, size, vector.ndim - 1)

    cw = jnp.concatenate([local(conv_w[:, :inner], width, me * width), conv_w[:, inner:]], axis=1)
    cb = jnp.concatenate([local(conv_b[:inner], width, me * width), conv_b[inner:]])[None]
    per_head = jnp.stack([local(p, heads, me * heads) for p in (dt_bias, a_log, skip_gain)])
    hp = jnp.pad(per_head, ((0, 5), (0, LANES - heads)))
    gain = local(gate_gain, width, me * width)[None]
    cols = 2 * width + 2 * STATE + LANES
    blocks = length // GROUP

    proj, y, core, opened = call(
        functools.partial(forward_kernel, heads),
        [
            ((length, cols), BF),
            ((length, width), BF),
            ((length, width), F32),
            ((blocks, STATE, width), F32),
        ],
        [((STATE, width), F32)],
        normed_all,
        w_all,
        cw,
        cb,
        hp,
    )
    dgated, stats = call(
        stats_kernel,
        [((length, width), F32), ((2, length), F32)],
        [],
        cot_all,
        wo,
        y,
        proj,
        gain,
    )
    stats = links.sum_axis(stats, "seq")
    out_part, gwo, dy, dz, ggain = call(
        functools.partial(gate_kernel, float(inner)),
        [
            ((length, depth), BF),
            ((width, depth), BF),
            ((length, width), BF),
            ((length, width), BF),
            ((1, width), F32),
        ],
        [((width, depth), F32)],
        cot_all,
        wo,
        y,
        proj,
        gain,
        dgated,
        stats,
    )
    dproj, gcw, gcb, ghp = call(
        functools.partial(backward_kernel, heads),
        [((length, cols), BF), ((CONV_W, chans), F32), ((1, chans), F32), ((8, LANES), F32)],
        [((STATE, width), F32), ((HALO, chans), F32)],
        proj,
        core,
        opened,
        dy,
        dz,
        cw,
        cb,
        hp,
    )

    block_out = residual + links.scatter_seq(out_part.reshape(seq, tokens, depth))
    gwo_rows = links.exchange_seq(gwo.reshape(width, seq, depth // seq).transpose(1, 0, 2))
    owned_w_out = links.scatter_fsdp(gwo_rows.reshape((fsdp,) + w_out.shape))

    shard = depth // fsdp
    dn_part = jnp.concatenate([dot(dproj, w_all[f], 1, 0).astype(BF) for f in range(fsdp)], axis=1)
    g_cols = [dot(dproj, normed_all[:, f * shard : (f + 1) * shard], 0, 0) for f in range(fsdp)]
    g_norm = jnp.concatenate(
        [jnp.sum(g_cols[f] * w_all[f].astype(F32), axis=0) for f in range(fsdp)]
    ) / norm_gain
    g_mine = links.scatter_fsdp(jnp.stack([g.astype(BF) for g in g_cols]))
    dnormed = links.scatter_seq(dn_part.reshape(seq, tokens, depth))
    dscaled = dnormed * norm_gain
    du_norm = scale * dscaled - residual * (
        scale * scale * scale * jnp.mean(residual * dscaled, axis=-1, keepdims=True)
    )
    grad_in = grad_out + du_norm

    g_half = g_mine.astype(BF)
    g_heads = dot(head_pick, g_half[2 * width + 2 * STATE :], 0, 0)[2 * STATE :]
    g_common = jnp.concatenate([g_half[2 * width : 2 * width + 2 * STATE], g_heads.astype(BF)])
    if links.pair == 2:
        other = lax.ppermute(g_common, "seq", [(i, i + 1) for i in range(0, seq, 2)])
        g_common = (g_common.astype(F32) + other.astype(F32)).astype(BF)
    g_pool = jnp.concatenate([g_half[: 2 * width], g_common], axis=0)
    sent = dot(one_hot(row_of(routes.back, me), routes.rows), g_pool, 1, 0).astype(BF)
    homed = [g_pool]
    for r, group in enumerate(routes.rounds):
        homed.append(
            lax.ppermute(sent[r * msg : (r + 1) * msg], "seq", [(p[1], p[0]) for p in group])
        )
    owned_w_in = dot(
        jnp.concatenate(homed, axis=0), one_hot(row_of(routes.home, me), w_in.shape[1]), 0, 0
    )

    def slot(value, size, at):
        zero = jnp.zeros(value.shape[:-1] + (size,), F32)
        return lax.dynamic_update_slice_in_dim(zero, value, at, value.ndim - 1)

    g_conv_w = jnp.concatenate([slot(gcw[:, :width], inner, me * width), gcw[:, width:]], axis=1)
    g_conv_b = jnp.concatenate([slot(gcb[0, :width], inner, me * width), gcb[0, width:]])
    pieces = [
        g_norm,
        g_conv_w.reshape(-1),
        g_conv_b,
        slot(ghp[0, :heads], heads_all, me * heads),
        slot(ghp[1, :heads], heads_all, me * heads),
        slot(ghp[2, :heads], heads_all, me * heads),
        slot(ggain[0], inner, me * width),
    ]
    sizes = [p.shape[0] for p in pieces]
    packed = jnp.concatenate(pieces)
    packed = jnp.pad(packed, (0, -packed.shape[0] % 1024)).reshape(-1, LANES)
    packed = links.sum_axis(links.sum_axis(packed, "seq"), "fsdp").reshape(-1)
    ends = np.cumsum([0] + sizes)
    summed = [packed[int(a) : int(b)] for a, b in zip(ends[:-1], ends[1:])]
    return (
        block_out[None],
        grad_in[None],
        summed[0],
        owned_w_in,
        summed[1].reshape(conv_w.shape),
        summed[2],
        summed[3],
        summed[4],
        summed[5],
        summed[6],
        owned_w_out,
    )


def dot_rows(w):
    return w.T


def solution(mesh):
    weights = P("fsdp", "seq")
    acts = P("fsdp", "seq", None)
    return jax.shard_map(
        functools.partial(per_device, mesh.shape["fsdp"], mesh.shape["seq"]),
        mesh=mesh,
        in_specs=(acts, P(), weights, P(), P(), P(), P(), P(), P(), weights, acts),
        out_specs=(acts, acts, P(), weights, P(), P(), P(), P(), P(), P(), weights),
        check_vma=False,
    )
```

```python
import functools

import jax
import jax.numpy as jnp
import numpy as np
from jax import lax
from jax.experimental import pallas as pl
from jax.experimental.pallas import tpu as pltpu
from jax.sharding import PartitionSpec as P


HEAD_DIM = 64
STATE = 128
CONV_W = 4
GROUP = 128
LANES = 128
EPS = 1e-05
HALO = 8
BF = jnp.bfloat16
F32 = jnp.float32
HIGH = lax.Precision.HIGHEST


def ceil_to(n, k):
    return (n + k - 1) // k * k


def dot(a, b, ca, cb, precision=None):
    return lax.dot_general(
        a, b, (((ca,), (cb,)), ((), ())), precision=precision, preferred_element_type=F32
    )


class Routes:
    def __init__(self, seq, columns, inner, state, heads):
        self.pair = 2 if seq % 2 == 0 else 1
        self.own = columns // seq
        self.width = inner // seq
        self.shared = 2 * state + heads
        width, own, pair = self.width, self.own, self.pair
        pieces = []
        for dst in range(seq):
            wants = [(dst * width, width, 0), (inner + dst * width, width, width)]
            if dst % pair == pair - 1:
                wants.append((2 * inner, self.shared, 2 * width))
            for start, length, at in wants:
                col = start
                while col < start + length:
                    src = col // own
                    stop = min(start + length, (src + 1) * own)
                    pieces.append((src, dst, col - src * own, stop - col, at + col - start))
                    col = stop
        self.local = [p for p in pieces if p[0] == p[1]]
        remote = [p for p in pieces if p[0] != p[1]]
        common = [p for p in remote if p[4] >= 2 * width]
        self.rounds = self.color(common) + self.color([p for p in remote if p[4] < 2 * width])
        self.sizes = [ceil_to(max(p[3] for p in group), 16) for group in self.rounds]
        self.starts = [sum(self.sizes[:r]) for r in range(len(self.sizes))]
        total = sum(self.sizes)
        self.rows = 2 * width + self.shared
        self.send = np.full((seq, total), -1, np.int32)
        self.take = np.full((seq, self.rows), -1, np.int32)
        self.back = np.full((seq, total), -1, np.int32)
        self.home = np.full((seq, self.rows + total), -1, np.int32)
        for src, dst, at, length, to in self.local:
            for i in range(length):
                self.take[dst, to + i] = at + i
                self.home[dst, to + i] = at + i
        for r, group in enumerate(self.rounds):
            for src, dst, at, length, to in group:
                first = self.starts[r]
                for i in range(length):
                    self.send[src, first + i] = at + i
                    self.take[dst, to + i] = own + first + i
                    self.back[dst, first + i] = to + i
                    self.home[src, self.rows + first + i] = at + i

    @staticmethod
    def color(pieces):
        rounds = []
        left = sorted(pieces, key=lambda p: -p[3])
        degree = {}
        for p in left:
            degree[("s", p[0])] = degree.get(("s", p[0]), 0) + 1
            degree[("d", p[1])] = degree.get(("d", p[1]), 0) + 1
        limit = max(degree.values()) if degree else 0
        used = {}
        colors = {}

        def free(node):
            taken = used.setdefault(node, {})
            return next(c for c in range(limit) if c not in taken)

        for index, p in enumerate(left):
            u, v = ("s", p[0]), ("d", p[1])
            a, b = free(u), free(v)
            if a != b and a in used[v]:
                path, node, want = [], v, a
                while want in used[node]:
                    edge = used[node][want]
                    path.append(edge)
                    q = left[edge]
                    ends = (("s", q[0]), ("d", q[1]))
                    node = ends[1] if node == ends[0] else ends[0]
                    want = b if want == a else a
                for edge in path:
                    q = left[edge]
                    for end in (("s", q[0]), ("d", q[1])):
                        used[end].pop(colors[edge], None)
                for edge in path:
                    q = left[edge]
                    colors[edge] = b if colors[edge] == a else a
                    for end in (("s", q[0]), ("d", q[1])):
                        used[end][colors[edge]] = edge
            colors[index] = a
            used[u][a] = index
            used[v][a] = index
        for c in range(limit):
            rounds.append([left[i] for i in range(len(left)) if colors[i] == c])
        return rounds


def one_hot(index, size):
    return (index[:, None] == lax.broadcasted_iota(jnp.int32, (index.shape[0], size), 1)).astype(BF)


class Links:
    def __init__(self, fsdp, seq):
        self.F, self.S = fsdp, seq
        self.pair = 2 if seq % 2 == 0 else 1
        self.chips = seq // self.pair
        self.f = lax.axis_index("fsdp")
        self.s = lax.axis_index("seq")
        self.chip = self.s // self.pair
        self.core = self.s % self.pair

    def swap(self, x):
        return lax.ppermute(x, "seq", [(i, i ^ 1) for i in range(self.S)])

    def hop(self, x, k):
        step = self.pair * k
        return lax.ppermute(x, "seq", [(i, (i + step) % self.S) for i in range(self.S)])

    def chip_at(self, k):
        return lax.rem(self.chip + k + self.chips, self.chips)

    def across(self, x, k):
        if self.F & (self.F - 1) == 0:
            pairs = [(i, i ^ k) for i in range(self.F)]
        else:
            pairs = [(i, (i + k) % self.F) for i in range(self.F)]
        return lax.ppermute(x, "fsdp", pairs)

    def gather_seq(self, x):
        mine, other = [x], []
        for k in range(1, self.chips):
            mine.append(self.hop(x, k))
        if self.pair == 2:
            for k in range(self.chips):
                other.append(self.swap(mine[k]))
        return mine + other

    def scatter_seq(self, keep, give, tokens):
        chips, rows, depth = keep.shape
        rows += rows - tokens
        if self.pair == 2:
            got = self.swap(give)
            own, *held = call(
                functools.partial(hold_kernel, tokens),
                [((rows, depth), F32)] + [((rows, depth), BF)] * (chips - 1),
                [],
                keep,
                got,
            )
        else:
            own, held = keep[0].astype(F32), [keep[k] for k in range(1, chips)]
        arrived = [own]
        for k in range(1, chips):
            arrived.append(self.hop(held[k - 1], k))
        return sum((a[:tokens].astype(F32) for a in arrived[1:]), own[:tokens]), arrived

    def exchange_seq(self, keep, give):
        if self.pair == 2:
            got = self.swap(give)
            first = self.core == 0
            parts = jnp.stack([jnp.where(first, keep, got), jnp.where(first, got, keep)], 1)
        else:
            parts = keep[:, None]
        out = [parts[0]]
        for k in range(1, self.chips):
            out.append(self.hop(parts[k], k))
        return out

    def gather_fsdp(self, x):
        out = [x]
        for k in range(1, self.F):
            out.append(self.across(x, k))
        return out

    def scatter_fsdp(self, parts):
        total = parts[0].astype(F32)
        for k in range(1, self.F):
            total = total + self.across(parts[k], k).astype(F32)
        return total

    def sum_axis(self, x, axis):
        size = self.S if axis == "seq" else self.F
        if size & (size - 1):
            return lax.psum(x, axis)
        k = 1
        while k < size:
            x = x + lax.ppermute(x, axis, [(i, i ^ k) for i in range(size)])
            k *= 2
        return x


def spread(values, heads):
    rows = values.shape[0]
    return jnp.concatenate(
        [jnp.broadcast_to(values[:, h : h + 1], (rows, HEAD_DIM)) for h in range(heads)], axis=1
    )


def widen(x):
    return jnp.concatenate([x, jnp.zeros((x.shape[0], LANES - x.shape[1]), x.dtype)], axis=1)


def softplus(x):
    return jnp.maximum(x, 0.0) + jnp.log1p(jnp.exp(-jnp.abs(x)))


def tri(lower):
    row = lax.broadcasted_iota(jnp.int32, (GROUP, GROUP), 0)
    col = lax.broadcasted_iota(jnp.int32, (GROUP, GROUP), 1)
    return (row >= col) if lower else (row <= col)


def conv_taps(v, halo):
    ext = jnp.concatenate([halo, v], axis=0)
    return [
        (pltpu.roll(ext, CONV_W - 1 - k, 0) if k < CONV_W - 1 else ext)[HALO:]
        for k in range(CONV_W)
    ]


def conv_pre(taps, cw, cb):
    pre = cb + cw[0:1] * taps[0]
    for k in range(1, CONV_W):
        pre = pre + cw[k : k + 1] * taps[k]
    return pre


def halo_of(proj_ref, i, lo, hi):
    start = pl.multiple_of(jnp.maximum(i * GROUP - 16, 0), 16)
    rows = proj_ref[pl.ds(start, 16), lo:hi].astype(F32)[16 - HALO :]
    return jnp.where(i > 0, rows, 0.0)


def peer_to(f, k, count):
    return lax.bitwise_xor(f, k) if count & (count - 1) == 0 else lax.rem(f + k, count)


def peer_from(f, k, count):
    if count & (count - 1) == 0:
        return lax.bitwise_xor(f, k)
    return lax.rem(f - k + count, count)


def spot(pair):
    me = lax.axis_index("seq")
    return me // pair, lax.rem(me, pair)


def assemble(pieces, whole_ref, chips, pair):
    tokens = whole_ref.shape[0] // (chips * pair)
    chip, core = spot(pair)
    for n, piece in enumerate(pieces):
        k, other = n % chips, n // chips
        at = lax.rem(chip - k + chips, chips) * pair + (1 - core if other else core)
        whole_ref[pl.ds(pl.multiple_of(at * tokens, tokens), tokens), :] = piece[...]


def columns_of(index, size):
    return pl.ds(pl.multiple_of(index * size, size), size)


def forward_kernel(heads, chips, pair, shards, *refs):
    pieces, refs = refs[: chips * pair], refs[chips * pair :]
    w_refs, refs = refs[:shards], refs[shards:]
    cw_ref, cb_ref, hp_ref, normed_ref, proj_ref, y_ref, core_ref, open_ref, state = refs
    width = heads * HEAD_DIM
    chans = width + 2 * STATE
    state[...] = jnp.zeros_like(state)
    depth = w_refs[0].shape[1]
    assemble(pieces, normed_ref, chips, pair)
    at = [peer_from(lax.axis_index("fsdp"), k, shards) for k in range(shards)]

    def step(i, _):
        rows = pl.ds(pl.multiple_of(i * GROUP, GROUP), GROUP)
        acc = dot(normed_ref[rows, columns_of(at[0], depth)], w_refs[0][...], 1, 1)
        for k in range(1, shards):
            acc = acc + dot(normed_ref[rows, columns_of(at[k], depth)], w_refs[k][...], 1, 1)
        proj = acc.astype(BF)
        proj_ref[rows, :] = proj
        v = proj[:, width : width + chans].astype(F32)
        taps = conv_taps(v, halo_of(proj_ref, i, width, width + chans))
        pre = conv_pre(taps, cw_ref[...], cb_ref[...])
        act = pre * jax.nn.sigmoid(pre)
        xs = act[:, :width]
        bs = act[:, width : width + STATE].astype(BF)
        cs = act[:, width + STATE :].astype(BF)
        dt = softplus(widen(proj[:, width + chans :].astype(F32)) + hp_ref[0:1])
        rate = -jnp.exp(hp_ref[1:2]) * dt
        run = dot(tri(True).astype(F32), rate, 1, 0, HIGH)
        run_t = run.T
        last = run[GROUP - 1 : GROUP]
        xdt = (xs * spread(dt, heads)).astype(BF)
        scores = dot(cs, bs, 1, 1)
        causal = tri(True)
        within = []
        for h in range(heads):
            gap = run[:, h : h + 1] - run_t[h : h + 1, :]
            decay = jnp.exp(jnp.where(causal, gap, -1e30))
            mixed = (scores * decay).astype(BF)
            within.append(dot(mixed, xdt[:, h * HEAD_DIM : (h + 1) * HEAD_DIM], 1, 0))
        memory = state[...]
        open_ref[i] = memory
        core = jnp.concatenate(within, axis=1) + spread(jnp.exp(run), heads) * dot(
            cs, memory.astype(BF), 1, 0
        )
        core_ref[rows, :] = core
        y_ref[rows, :] = (core + spread(hp_ref[2:3], heads) * xs).astype(BF)
        toward = (xdt.astype(F32) * spread(jnp.exp(last - run), heads)).astype(BF)
        state[...] = spread(jnp.exp(last), heads) * memory + dot(bs, toward, 0, 0)
        return 0

    lax.fori_loop(0, normed_ref.shape[0] // GROUP, step, 0, unroll=2)


def stats_kernel(chips, pair, *refs):
    pieces, refs = refs[: chips * pair], refs[chips * pair :]
    wo_refs, refs = refs[:chips], refs[chips:]
    y_ref, proj_ref, gain_ref, cot_ref, wo_ref, dg_ref, stats_ref = refs
    width = y_ref.shape[1]
    ones = jnp.ones((8, width), F32)
    assemble(pieces, cot_ref, chips, pair)
    part = wo_refs[0].shape[1]
    for k in range(chips):
        for core in range(pair):
            src = lax.rem(spot(pair)[0] - k + chips, chips) * pair + core
            wo_ref[pl.ds(pl.multiple_of(src * part, part), part), :] = wo_refs[k][core]

    def step(i, _):
        rows = pl.ds(pl.multiple_of(i * GROUP, GROUP), GROUP)
        dg = dot(cot_ref[rows, :], wo_ref[...], 1, 0)
        dg_ref[rows, :] = dg
        z = proj_ref[rows, :width].astype(F32)
        u = y_ref[rows, :].astype(F32) * (z * jax.nn.sigmoid(z))
        stats_ref[0:1, rows] = dot(ones, u * u, 1, 1, HIGH)[0:1]
        stats_ref[1:2, rows] = dot(ones, u * gain_ref[...] * dg, 1, 1, HIGH)[0:1]
        return 0

    lax.fori_loop(0, cot_ref.shape[0] // GROUP, step, 0, unroll=4)


def gate_kernel(
    inner,
    chips,
    pair,
    cot_ref,
    wo_ref,
    y_ref,
    proj_ref,
    gain_ref,
    dg_ref,
    stats_ref,
    *refs,
):
    out_refs, refs = refs[:pair], refs[pair:]
    gwo_refs, (dy_ref, dz_ref, ggain_ref, acc) = refs[:-4], refs[-4:]
    width = y_ref.shape[1]
    tokens = cot_ref.shape[0] // (chips * pair)
    part = wo_ref.shape[0] // (chips * pair)
    acc[...] = jnp.zeros_like(acc)
    ggain_ref[...] = jnp.zeros_like(ggain_ref)
    gain = gain_ref[...]
    chip, core = spot(pair)

    def device(k, other):
        return lax.rem(chip + k, chips) * pair + (1 - core if other else core)

    def step(k, _):
        for other in range(pair):
            rows = columns_of(device(k, other), tokens)
            st = jnp.concatenate([stats_ref[:, rows], jnp.zeros((6, tokens), F32)], axis=0).T
            r = lax.rsqrt(st[:, 0:1] / inner + EPS)
            y = y_ref[rows, :].astype(F32)
            z = proj_ref[rows, :width].astype(F32)
            sig = jax.nn.sigmoid(z)
            sz = z * sig
            u = y * sz
            dg = dg_ref[rows, :]
            ur = u * r
            gated = (ur * gain).astype(BF)
            du = r * (gain * dg) - u * (r * r * r * (st[:, 1:2] / inner))
            ggain_ref[...] += jnp.sum(dg * ur, axis=0, keepdims=True)
            dy_ref[rows, :] = (du * sz).astype(BF)
            dz_ref[rows, :] = (du * y * (sig * (1.0 + z * (1.0 - sig)))).astype(BF)
            out_refs[other][k, :tokens] = dot(gated, wo_ref[...], 1, 1).astype(BF)
            acc[...] += dot(cot_ref[rows, :], gated, 0, 0)
        return 0

    lax.fori_loop(0, chips, step, 0, unroll=2)
    for k in range(chips):
        for other in range(pair):
            piece = acc[columns_of(device(k, other), part), :].astype(BF)
            if gwo_refs:
                gwo_refs[other][k] = piece
                continue
            rows = out_refs[other].shape[1] - tokens
            for j in range(part // rows):
                lanes = slice(j * width, (j + 1) * width)
                out_refs[other][k, tokens:, lanes] = piece[j * rows : (j + 1) * rows]


def backward_kernel(
    heads,
    chips,
    pair,
    shards,
    proj_ref,
    core_ref,
    open_ref,
    dy_ref,
    dz_ref,
    cw_ref,
    cb_ref,
    hp_ref,
    *refs,
):
    w_refs, refs = refs[:shards], refs[shards:]
    dn_refs, refs = refs[:pair], refs[pair:]
    dproj_ref, gcw_ref, gcb_ref, ghp_ref, dstate, ahead = refs
    shard = w_refs[0].shape[1]
    tokens = proj_ref.shape[0] // (chips * pair)
    per = tokens // GROUP
    at = [peer_from(lax.axis_index("fsdp"), k, shards) for k in range(shards)]
    chip, core = spot(pair)
    width = heads * HEAD_DIM
    chans = width + 2 * STATE
    blocks = proj_ref.shape[0] // GROUP
    dstate[...] = jnp.zeros_like(dstate)
    ahead[...] = jnp.zeros_like(ahead)
    gcw_ref[...] = jnp.zeros_like(gcw_ref)
    gcb_ref[...] = jnp.zeros_like(gcb_ref)
    ghp_ref[...] = jnp.zeros_like(ghp_ref)
    fold = (
        lax.broadcasted_iota(jnp.int32, (width, LANES), 0) // HEAD_DIM
        == lax.broadcasted_iota(jnp.int32, (width, LANES), 1)
    ).astype(F32)

    def step(n, _):
        i = blocks - 1 - n
        rows = pl.ds(pl.multiple_of(i * GROUP, GROUP), GROUP)
        v = proj_ref[rows, width : width + chans].astype(F32)
        taps = conv_taps(v, halo_of(proj_ref, i, width, width + chans))
        cw = cw_ref[...]
        pre = conv_pre(taps, cw, cb_ref[...])
        sig = jax.nn.sigmoid(pre)
        act = pre * sig
        xs = act[:, :width]
        bs = act[:, width : width + STATE].astype(BF)
        cs = act[:, width + STATE :].astype(BF)
        shifted = widen(proj_ref[rows, width + chans :].astype(F32)) + hp_ref[0:1]
        dt = softplus(shifted)
        neg = -jnp.exp(hp_ref[1:2])
        rate = neg * dt
        run = dot(tri(True).astype(F32), rate, 1, 0, HIGH)
        run_t = run.T
        last = run[GROUP - 1 : GROUP]
        dt_x = spread(dt, heads)
        xdt = (xs * dt_x).astype(BF)
        scores = dot(cs, bs, 1, 1)
        causal = tri(True)
        dyb = dy_ref[rows, :]
        dy = dyb.astype(F32)
        dscores = jnp.zeros((GROUP, GROUP), F32)
        parts = []
        for h in range(heads):
            cols = slice(h * HEAD_DIM, (h + 1) * HEAD_DIM)
            gap = run[:, h : h + 1] - run_t[h : h + 1, :]
            decay = jnp.exp(jnp.where(causal, gap, -1e30))
            mixed = (scores * decay).astype(BF)
            parts.append(dot(mixed, dyb[:, cols], 0, 0))
            dscores = dscores + dot(dyb[:, cols], xdt[:, cols], 1, 1) * decay
        dscores = dscores.astype(BF)
        memory = open_ref[i]
        mem_b = memory.astype(BF)
        ds = dstate[...]
        ds_b = ds.astype(BF)
        edy = (spread(jnp.exp(run), heads) * dy).astype(BF)
        dec = spread(jnp.exp(last - run), heads)
        xdt_f = xdt.astype(F32)
        inflow = dec * dot(bs, ds_b, 1, 0)
        dxdt = jnp.concatenate(parts, axis=1) + inflow
        dc = dot(dscores, bs, 1, 0) + dot(edy, mem_b, 1, 1)
        db = dot(dscores, cs, 0, 0) + dot((xdt_f * dec).astype(BF), ds_b, 1, 1)
        carried = spread(jnp.exp(last), heads)
        dstate[...] = dot(cs, edy, 0, 0) + carried * ds
        dx = dt_x * dxdt + spread(hp_ref[2:3], heads) * dy
        tops = jnp.concatenate(
            [
                jnp.sum(xdt_f * inflow, axis=0, keepdims=True)
                + carried * jnp.sum(ds * memory, axis=0, keepdims=True),
                jnp.sum(dy * xs, axis=0, keepdims=True),
                jnp.zeros((6, width), F32),
            ],
            axis=0,
        )
        folded = dot(
            jnp.concatenate([xs * dxdt, dy * core_ref[rows, :] - xdt_f * dxdt, tops], axis=0),
            fold,
            1,
            0,
            HIGH,
        )
        dend = folded[2 * GROUP : 2 * GROUP + 1]
        drate = dot(tri(False).astype(F32), folded[GROUP : 2 * GROUP], 1, 0, HIGH) + dend
        ddt = folded[:GROUP] + neg * drate
        ddtr = ddt * jax.nn.sigmoid(shifted)
        ghp_ref[0:1] += jnp.sum(ddtr, axis=0, keepdims=True)
        ghp_ref[1:2] += jnp.sum(drate * rate, axis=0, keepdims=True)
        ghp_ref[2:3] += folded[2 * GROUP + 1 : 2 * GROUP + 2]
        dact = jnp.concatenate([dx, db, dc], axis=1)
        dpre = dact * (sig * (1.0 + pre * (1.0 - sig)))
        gcb_ref[...] += jnp.sum(dpre, axis=0, keepdims=True)
        for k in range(CONV_W):
            gcw_ref[k : k + 1] += jnp.sum(dpre * taps[k], axis=0, keepdims=True)
        ext = jnp.concatenate([dpre, ahead[...]], axis=0)
        ahead[...] = dpre[:HALO]
        dv = cw[CONV_W - 1 :] * dpre
        for k in range(CONV_W - 1):
            moved = pltpu.roll(ext, ext.shape[0] - (CONV_W - 1 - k), 0)[:GROUP]
            dv = dv + cw[k : k + 1] * moved
        few = dproj_ref.shape[1] - width - chans
        dproj = jnp.concatenate(
            [dz_ref[rows, :], dv.astype(BF), ddtr[:, :few].astype(BF)], axis=1
        )
        dproj_ref[rows, :] = dproj
        owner = i // per
        k = lax.rem(owner // pair - chip + chips, chips)
        inside = pl.ds(pl.multiple_of((i % per) * GROUP, GROUP), GROUP)
        dn = [dot(dproj, w[...], 1, 0).astype(BF) for w in w_refs]
        for other in range(pair):

            @pl.when((owner % pair != core) == bool(other))
            def _():
                for j in range(shards):
                    dn_refs[other][k, inside, columns_of(at[j], shard)] = dn[j]

        return 0

    lax.fori_loop(0, blocks, step, 0, unroll=2)


def columns_kernel(heads, shards, dproj_ref, normed_ref, *refs):
    w_refs, refs = refs[:shards], refs[shards:]
    gcw_ref, gcb_ref, ghp_ref, ggain_ref, refs = *refs[:4], refs[4:]
    g_refs, (gnorm_ref, slots_ref, common_ref) = refs[:shards], refs[shards:]
    width = ggain_ref.shape[1]
    lanes = min(width, LANES)
    packed = ghp_ref[0:1]
    for n in range(1, 3):
        packed = packed + pltpu.roll(ghp_ref[n : n + 1], n * heads, 1)
    packed = packed[:, :lanes]
    if lanes < width:
        packed = jnp.concatenate([packed, jnp.zeros((1, width - lanes), F32)], axis=1)
    slots_ref[...] = jnp.zeros_like(slots_ref)
    slots_ref[lax.axis_index("seq")] = jnp.concatenate(
        [
            gcw_ref[:, :width],
            gcb_ref[:, :width],
            ggain_ref[...],
            packed,
            jnp.zeros((1, width), F32),
        ],
        axis=0,
    )
    common_ref[...] = jnp.concatenate(
        [gcw_ref[:, width:], gcb_ref[:, width:], jnp.zeros((3, 2 * STATE), F32)], axis=0
    )
    shard = w_refs[0].shape[1]
    for k in range(shards):
        at = columns_of(peer_to(lax.axis_index("fsdp"), k, shards), shard)
        g = dot(dproj_ref[...], normed_ref[:, at], 0, 0)
        g_refs[k][...] = g.astype(BF)
        source = peer_index(k, shards)
        gnorm_ref[0:1, at] = jnp.sum(g * w_refs[source][...].astype(F32), axis=0, keepdims=True)


def chosen(index, start, size):
    row = lax.broadcasted_iota(jnp.int32, (size, index.shape[1]), 0) + start
    return (row == index).astype(F32).astype(BF)


def table_row(table_ref):
    return table_ref[pl.ds(lax.axis_index("seq"), 1), :]


def pick_kernel(table_ref, w_ref, *out_refs):
    index, start = table_row(table_ref), 0
    for out_ref in out_refs:
        items = index[:, start : start + out_ref.shape[0]]
        out_ref[...] = dot(chosen(items, 0, w_ref.shape[0]), w_ref[...], 0, 0).astype(BF)
        start += out_ref.shape[0]


def place_kernel(table_ref, w_ref, *refs):
    arrived, out_ref = refs[:-1], refs[-1]
    index, start, out = table_row(table_ref), 0, None
    for piece in (w_ref, *arrived):
        part = dot(chosen(index, start, piece.shape[0]), piece[...], 0, 0)
        out = part if out is None else out + part
        start += piece.shape[0]
    out_ref[...] = out.astype(BF)


def back_kernel(table_ref, g_ref, common_ref, pool_ref, *out_refs):
    split = pool_ref.shape[0] - common_ref.shape[0]
    pool_ref[:split] = g_ref[:split]
    pool_ref[split:] = common_ref[...]
    index, start = table_row(table_ref), 0
    for out_ref in out_refs:
        items = index[:, start : start + out_ref.shape[0]]
        out_ref[...] = dot(chosen(items, 0, pool_ref.shape[0]), pool_ref[...], 0, 0).astype(BF)
        start += out_ref.shape[0]


def home_kernel(table_ref, *refs):
    pieces, out_ref = refs[:-1], refs[-1]
    index, start, out = table_row(table_ref), 0, None
    for piece in pieces:
        items = index[:, start : start + piece.shape[0]]
        part = dot(chosen(items, 0, out_ref.shape[0]), piece[...], 1, 0)
        out = part if out is None else out + part
        start += piece.shape[0]
    out_ref[...] = out


def hold_kernel(tokens, keep_ref, got_ref, own_ref, *out_refs):
    rows = keep_ref.shape[1]
    for k in range(keep_ref.shape[0]):
        total = keep_ref[k, :tokens].astype(F32) + got_ref[k, :tokens].astype(F32)
        if k == 0:
            own_ref[:tokens] = total
        else:
            out_refs[k - 1][:tokens] = total.astype(BF)
        if rows > tokens:
            extra = rows - tokens
            for n, ref in enumerate((keep_ref, got_ref)):
                at = slice(tokens + n * extra, tokens + (n + 1) * extra)
                if k == 0:
                    own_ref[at] = ref[k, tokens:].astype(F32)
                else:
                    out_refs[k - 1][at] = ref[k, tokens:]


def peer_index(k, count):
    return k if count & (count - 1) == 0 else (count - k) % count


def call(kernel, outs, scratch, *args):
    whole = pl.BlockSpec(memory_space=pltpu.VMEM)
    return pl.pallas_call(
        kernel,
        out_shape=[jax.ShapeDtypeStruct(shape, kind) for shape, kind in outs],
        in_specs=[whole] * len(args),
        out_specs=[whole] * len(outs),
        scratch_shapes=[pltpu.VMEM(shape, kind) for shape, kind in scratch],
    )(*args)


def per_device(
    fsdp,
    seq,
    block_input,
    norm_gain,
    w_in,
    conv_w,
    conv_b,
    dt_bias,
    a_log,
    skip_gain,
    gate_gain,
    w_out,
    out_cotangent,
):
    links = Links(fsdp, seq)
    residual = block_input[0]
    grad_out = out_cotangent[0]
    tokens, depth = residual.shape
    length = tokens * seq
    heads_all = dt_bias.shape[0]
    inner = gate_gain.shape[0]
    heads = heads_all // seq
    width = inner // seq
    chans = width + 2 * STATE
    routes = Routes(seq, w_in.shape[1] * seq, inner, STATE, heads_all)
    me = links.s
    shared = routes.shared

    mean = jnp.mean(residual * residual, axis=-1, keepdims=True)
    scale = lax.rsqrt(mean + EPS)
    normed_half = (residual * scale * norm_gain).astype(BF)

    w_cols = w_in.T
    rows_here = w_in.shape[0]
    picked = call(
        pick_kernel,
        [((size, rows_here), BF) for size in routes.sizes],
        [],
        jnp.asarray(routes.send),
        w_cols,
    )
    arrived = []
    for r, group in enumerate(routes.rounds):
        arrived.append(lax.ppermute(picked[r], "seq", [(p[0], p[1]) for p in group]))
    (mine,) = call(
        place_kernel,
        [((routes.rows, rows_here), BF)],
        [],
        jnp.asarray(routes.take),
        w_cols,
        *arrived,
    )
    common = mine[2 * width :]
    if links.pair == 2:
        common = common + lax.ppermute(
            common, "seq", [(i, i - 1) for i in range(1, seq, 2)]
        )
    head_row = jnp.arange(ceil_to(heads, 16), dtype=jnp.int32)
    head_row = jnp.where(head_row < heads, 2 * STATE + me * heads + head_row, -1)
    head_pick = one_hot(head_row, shared)
    w_mine = jnp.concatenate(
        [mine[: 2 * width], common[: 2 * STATE], dot(head_pick, common, 1, 0).astype(BF)], axis=0
    )
    normed = links.gather_seq(normed_half)
    w_all = links.gather_fsdp(w_mine)

    wo_half = w_out.reshape(-1, width, w_out.shape[1]).transpose(0, 2, 1)
    wo_rows = jnp.zeros((fsdp,) + wo_half.shape, BF)
    for k, piece in enumerate(links.gather_fsdp(wo_half)):
        wo_rows = lax.dynamic_update_index_in_dim(wo_rows, piece, peer_from(links.f, k, fsdp), 0)
    wo_rows = wo_rows.reshape((links.chips, links.pair) + wo_half.shape[1:])
    order = [links.chip_at(k) for k in range(links.chips)]

    def parity(core):
        picks = [lax.dynamic_slice(wo_rows, (c, core, 0, 0), (1, 1) + wo_half.shape[1:]) for c in order]
        return jnp.concatenate(picks, axis=0)[:, 0]

    wo = links.exchange_seq(parity(links.core), parity(1 - links.core))
    cot_half = grad_out.astype(BF)
    cot_half, _ = lax.optimization_barrier((cot_half, tuple(normed)))
    cot = links.gather_seq(cot_half)

    def local(vector, size, start):
        return lax.dynamic_slice_in_dim(vector, start, size, vector.ndim - 1)

    cw = jnp.concatenate([local(conv_w[:, :inner], width, me * width), conv_w[:, inner:]], axis=1)
    cb = jnp.concatenate([local(conv_b[:inner], width, me * width), conv_b[inner:]])[None]
    per_head = jnp.stack([local(p, heads, me * heads) for p in (dt_bias, a_log, skip_gain)])
    hp = jnp.pad(per_head, ((0, 5), (0, LANES - heads)))
    gain = local(gate_gain, width, me * width)[None]
    narrow = ceil_to(heads, 16)
    cols = 2 * width + 2 * STATE + narrow
    blocks = length // GROUP

    chips, pair = links.chips, links.pair
    normed_all, proj, y, core, opened = call(
        functools.partial(forward_kernel, heads, chips, pair, fsdp),
        [
            ((length, depth), BF),
            ((length, cols), BF),
            ((length, width), BF),
            ((length, width), F32),
            ((blocks, STATE, width), F32),
        ],
        [((STATE, width), F32)],
        *normed,
        *w_all,
        cw,
        cb,
        hp,
    )
    cot_all, wo_all, dgated, stats = call(
        functools.partial(stats_kernel, chips, pair),
        [((length, depth), BF), ((depth, width), BF), ((length, width), F32), ((2, length), F32)],
        [],
        *cot,
        *wo,
        y,
        proj,
        gain,
    )
    stats = links.sum_axis(stats, "seq")
    halves = [((chips, tokens, depth), BF)] * pair
    part = depth // seq
    extra = part * width // depth
    together = pair == 2 and extra % 16 == 0 and width % LANES == 0
    out_halves = [((chips, tokens + extra, depth), BF)] * pair if together else halves
    quarters = [] if together else [((chips, part, width), BF)] * pair
    gate_outs = call(
        functools.partial(gate_kernel, float(inner), chips, pair),
        out_halves
        + quarters
        + [((length, width), BF), ((length, width), BF), ((1, width), F32)],
        [((depth, width), F32)],
        cot_all,
        wo_all,
        y,
        proj,
        gain,
        dgated,
        stats,
    )
    out_halves, gwo_halves = gate_outs[:pair], gate_outs[pair:-3]
    dy, dz, ggain = gate_outs[-3:]
    back_outs = call(
        functools.partial(backward_kernel, heads, chips, pair, fsdp),
        halves
        + [((length, cols), BF), ((CONV_W, chans), F32), ((1, chans), F32), ((8, LANES), F32)],
        [((STATE, width), F32), ((HALO, chans), F32)],
        proj,
        core,
        opened,
        dy,
        dz,
        cw,
        cb,
        hp,
        *w_all,
    )
    dn_halves = back_outs[:pair]
    dproj, gcw, gcb, ghp = back_outs[pair:]
    shard = depth // fsdp
    *g_cols, g_norm, slots, g_shared = call(
        functools.partial(columns_kernel, heads, fsdp),
        [((cols, shard), BF)] * fsdp
        + [((1, depth), F32), ((seq, 8, width), F32), ((8, 2 * STATE), F32)],
        [],
        dproj,
        normed_all,
        *w_all,
        gcw,
        gcb,
        ghp,
        ggain,
    )

    out_sum, arrived = links.scatter_seq(out_halves[0], out_halves[-1], tokens)
    block_out = residual + out_sum
    if together:
        gwo = []
        for piece in arrived:
            both = piece[tokens:].astype(BF).reshape(2, extra, part // extra, width)
            both = both.transpose(0, 2, 1, 3).reshape(2, part, width)
            gwo.append(jnp.where(links.core == 0, both, both[::-1]))
    else:
        gwo = links.exchange_seq(gwo_halves[0], gwo_halves[-1])
    gwo_rows = jnp.zeros((chips,) + gwo[0].shape, BF)
    for k, piece in enumerate(gwo):
        gwo_rows = lax.dynamic_update_index_in_dim(gwo_rows, piece, links.chip_at(-k), 0)
    gwo_rows = gwo_rows.reshape((fsdp, seq // fsdp, depth // seq, width))
    to = [
        lax.dynamic_index_in_dim(gwo_rows, peer_to(links.f, k, fsdp), 0, keepdims=False)
        for k in range(fsdp)
    ]
    owned_w_out = links.scatter_fsdp(to).transpose(0, 2, 1).reshape(w_out.shape)

    g_mine = links.scatter_fsdp(g_cols)
    dnormed, dn_arrived = links.scatter_seq(dn_halves[0], dn_halves[-1], tokens)
    dscaled = dnormed * norm_gain
    du_norm = scale * dscaled - residual * (
        scale * scale * scale * jnp.mean(residual * dscaled, axis=-1, keepdims=True)
    )
    grad_in = grad_out + du_norm

    g_half = g_mine.astype(BF)
    g_heads = dot(head_pick, g_half[2 * width + 2 * STATE :], 0, 0)[2 * STATE :]
    g_common = jnp.concatenate([g_half[2 * width : 2 * width + 2 * STATE], g_heads.astype(BF)])
    if links.pair == 2:
        other = lax.ppermute(g_common, "seq", [(i, i + 1) for i in range(0, seq, 2)])
        g_common = (g_common.astype(F32) + other.astype(F32)).astype(BF)
    g_pool, *sent = call(
        back_kernel,
        [((routes.rows, rows_here), BF)] + [((size, rows_here), BF) for size in routes.sizes],
        [],
        jnp.asarray(routes.back),
        g_half,
        g_common,
    )
    homed = []
    for r, group in enumerate(routes.rounds):
        homed.append(lax.ppermute(sent[r], "seq", [(p[1], p[0]) for p in group]))
    (owned_w_in,) = call(
        home_kernel, [(w_cols.shape, F32)], [], jnp.asarray(routes.home), g_pool, *homed
    )
    owned_w_in = owned_w_in.T

    pieces, _ = lax.optimization_barrier(([slots, g_shared, g_norm], dn_arrived[0]))
    packed = jnp.concatenate([p.reshape(-1, LANES) for p in pieces], axis=0)
    packed = links.sum_axis(packed, "seq")
    packed = links.sum_axis(packed, "fsdp")
    first = slots.size // LANES
    slots = packed[:first].reshape(slots.shape)
    second = first + g_shared.size // LANES
    g_shared = packed[first:second].reshape(g_shared.shape)
    g_norm = packed[second:].reshape(-1) / norm_gain
    g_conv_w = jnp.concatenate(
        [slots[:, :CONV_W].transpose(1, 0, 2).reshape(CONV_W, inner), g_shared[:CONV_W]], axis=1
    )
    g_conv_b = jnp.concatenate([slots[:, CONV_W].reshape(inner), g_shared[CONV_W]])
    g_gain = slots[:, CONV_W + 1].reshape(inner)
    g_head = [slots[:, CONV_W + 2, n * heads : (n + 1) * heads].reshape(-1) for n in range(3)]
    return (
        block_out[None],
        grad_in[None],
        g_norm,
        owned_w_in,
        g_conv_w,
        g_conv_b,
        *g_head,
        g_gain,
        owned_w_out,
    )


def solution(mesh):
    weights = P("fsdp", "seq")
    acts = P("fsdp", "seq", None)
    fsdp, seq = mesh.shape["fsdp"], mesh.shape["seq"]

    def body(*args):
        return per_device(fsdp, seq, *args)

    return jax.shard_map(
        body,
        mesh=mesh,
        in_specs=(acts, P(), weights, P(), P(), P(), P(), P(), P(), weights, acts),
        out_specs=(acts, acts, P(), weights, P(), P(), P(), P(), P(), P(), weights),
        check_vma=False,
    )
```

```python
import functools

import jax
import jax.numpy as jnp
import numpy as np
from jax import lax
from jax.experimental import pallas as pl
from jax.experimental.pallas import tpu as pltpu
from jax.sharding import PartitionSpec as P


HEAD_DIM = 64
STATE = 128
CONV_W = 4
GROUP = 128
LANES = 128
EPS = 1e-05
HALO = 8
BF = jnp.bfloat16
F32 = jnp.float32


def ceil_to(n, k):
    return (n + k - 1) // k * k


def dot(a, b, ca, cb):
    return lax.dot_general(a, b, (((ca,), (cb,)), ((), ())), preferred_element_type=F32)


def thirds(x):
    parts = []
    for _ in range(3):
        part = x.astype(BF)
        parts.append(part)
        x = x - part.astype(F32)
    return parts


def pick_sums(picks, x, cp, cx, first=True):
    if first:
        return sum(dot(picks, part, cp, cx) for part in thirds(x))
    return sum(dot(part, picks, cx, cp) for part in thirds(x))


class Routes:
    def __init__(self, seq, columns, inner, state, heads):
        self.pair = 2 if seq % 2 == 0 else 1
        self.own = columns // seq
        self.width = inner // seq
        self.shared = 2 * state + heads
        width, own, pair = self.width, self.own, self.pair
        pieces = []
        for dst in range(seq):
            wants = [(dst * width, width, 0), (inner + dst * width, width, width)]
            if dst % pair == pair - 1:
                wants.append((2 * inner, self.shared, 2 * width))
            for start, length, at in wants:
                col = start
                while col < start + length:
                    src = col // own
                    stop = min(start + length, (src + 1) * own)
                    pieces.append((src, dst, col - src * own, stop - col, at + col - start))
                    col = stop
        self.local = [p for p in pieces if p[0] == p[1]]
        remote = [p for p in pieces if p[0] != p[1]]
        common = [p for p in remote if p[4] >= 2 * width]
        self.rounds = self.color(common) + self.color([p for p in remote if p[4] < 2 * width])
        self.kinds = [group[0][4] >= 2 * width for group in self.rounds]
        self.sizes = [ceil_to(max(p[3] for p in group), 16) for group in self.rounds]
        self.starts = [sum(self.sizes[:r]) for r in range(len(self.sizes))]
        total = sum(self.sizes)
        self.rows = 2 * width + self.shared
        self.send = np.full((seq, total), -1, np.int32)
        self.take = np.full((seq, self.rows), -1, np.int32)
        self.back = np.full((seq, total), -1, np.int32)
        self.home = np.full((seq, self.rows + total), -1, np.int32)
        for src, dst, at, length, to in self.local:
            for i in range(length):
                self.take[dst, to + i] = at + i
                self.home[dst, to + i] = at + i
        for r, group in enumerate(self.rounds):
            for src, dst, at, length, to in group:
                first = self.starts[r]
                for i in range(length):
                    self.send[src, first + i] = at + i
                    self.take[dst, to + i] = own + first + i
                    self.back[dst, first + i] = to + i
                    self.home[src, self.rows + first + i] = at + i

    @staticmethod
    def color(pieces):
        rounds = []
        left = sorted(pieces, key=lambda p: -p[3])
        degree = {}
        for p in left:
            degree[("s", p[0])] = degree.get(("s", p[0]), 0) + 1
            degree[("d", p[1])] = degree.get(("d", p[1]), 0) + 1
        limit = max(degree.values()) if degree else 0
        used = {}
        colors = {}

        def free(node):
            taken = used.setdefault(node, {})
            return next(c for c in range(limit) if c not in taken)

        for index, p in enumerate(left):
            u, v = ("s", p[0]), ("d", p[1])
            a, b = free(u), free(v)
            if a != b and a in used[v]:
                path, node, want = [], v, a
                while want in used[node]:
                    edge = used[node][want]
                    path.append(edge)
                    q = left[edge]
                    ends = (("s", q[0]), ("d", q[1]))
                    node = ends[1] if node == ends[0] else ends[0]
                    want = b if want == a else a
                for edge in path:
                    q = left[edge]
                    for end in (("s", q[0]), ("d", q[1])):
                        used[end].pop(colors[edge], None)
                for edge in path:
                    q = left[edge]
                    colors[edge] = b if colors[edge] == a else a
                    for end in (("s", q[0]), ("d", q[1])):
                        used[end][colors[edge]] = edge
            colors[index] = a
            used[u][a] = index
            used[v][a] = index
        for c in range(limit):
            rounds.append([left[i] for i in range(len(left)) if colors[i] == c])
        return rounds


def one_hot(index, size):
    return (index[:, None] == lax.broadcasted_iota(jnp.int32, (index.shape[0], size), 1)).astype(BF)


class Links:
    def __init__(self, fsdp, seq):
        self.F, self.S = fsdp, seq
        self.pair = 2 if seq % 2 == 0 else 1
        self.chips = seq // self.pair
        self.f = lax.axis_index("fsdp")
        self.s = lax.axis_index("seq")
        self.chip = self.s // self.pair
        self.core = self.s % self.pair

    def swap(self, x):
        return lax.ppermute(x, "seq", [(i, i ^ 1) for i in range(self.S)])

    def hop(self, x, k):
        step = self.pair * k
        return lax.ppermute(x, "seq", [(i, (i + step) % self.S) for i in range(self.S)])

    def chip_at(self, k):
        return lax.rem(self.chip + k + self.chips, self.chips)

    def across(self, x, k):
        if self.F & (self.F - 1) == 0:
            pairs = [(i, i ^ k) for i in range(self.F)]
        else:
            pairs = [(i, (i + k) % self.F) for i in range(self.F)]
        return lax.ppermute(x, "fsdp", pairs)

    def gather_seq(self, x):
        mine, other = [x], []
        for k in range(1, self.chips):
            mine.append(self.hop(x, k))
        if self.pair == 2:
            for k in range(self.chips):
                other.append(self.swap(mine[k]))
        return mine + other

    def scatter_seq(self, keep, give, tokens):
        chips, rows, depth = keep.shape
        rows += rows - tokens
        if self.pair == 2:
            got = self.swap(give)
            own, *held = call(
                functools.partial(hold_kernel, tokens),
                [((rows, depth), F32)] + [((rows, depth), BF)] * (chips - 1),
                [],
                keep,
                got,
            )
        else:
            own, held = keep[0].astype(F32), [keep[k] for k in range(1, chips)]
        arrived = [own]
        for k in range(1, chips):
            arrived.append(self.hop(held[k - 1], k))
        return sum((a[:tokens].astype(F32) for a in arrived[1:]), own[:tokens]), arrived

    def exchange_seq(self, keep, give):
        if self.pair == 2:
            got = self.swap(give)
            first = self.core == 0
            parts = jnp.stack([jnp.where(first, keep, got), jnp.where(first, got, keep)], 1)
        else:
            parts = keep[:, None]
        out = [parts[0]]
        for k in range(1, self.chips):
            out.append(self.hop(parts[k], k))
        return out

    def gather_fsdp(self, x):
        out = [x]
        for k in range(1, self.F):
            out.append(self.across(x, k))
        return out

    def scatter_fsdp(self, parts):
        total = parts[0].astype(F32)
        for k in range(1, self.F):
            total = total + self.across(parts[k], k).astype(F32)
        return total

    def sum_seq(self, x):
        if self.pair == 2:
            x = x + self.swap(x)
        total = x
        for k in range(1, self.chips):
            total = total + self.hop(x, k)
        return total

    def sum_fsdp(self, x):
        total = x
        for k in range(1, self.F):
            total = total + self.across(x, k)
        return total


def spread(values, heads):
    rows = values.shape[0]
    return jnp.concatenate(
        [jnp.broadcast_to(values[:, h : h + 1], (rows, HEAD_DIM)) for h in range(heads)], axis=1
    )


def widen(x):
    return jnp.concatenate([x, jnp.zeros((x.shape[0], LANES - x.shape[1]), x.dtype)], axis=1)


def softplus(x):
    return jnp.maximum(x, 0.0) + jnp.log1p(jnp.exp(-jnp.abs(x)))


def tri(lower):
    row = lax.broadcasted_iota(jnp.int32, (GROUP, GROUP), 0)
    col = lax.broadcasted_iota(jnp.int32, (GROUP, GROUP), 1)
    return (row >= col) if lower else (row <= col)


def conv_taps(v, halo):
    ext = jnp.concatenate([halo, v], axis=0)
    return [
        (pltpu.roll(ext, CONV_W - 1 - k, 0) if k < CONV_W - 1 else ext)[HALO:]
        for k in range(CONV_W)
    ]


def conv_pre(taps, cw, cb):
    pre = cb + cw[0:1] * taps[0]
    for k in range(1, CONV_W):
        pre = pre + cw[k : k + 1] * taps[k]
    return pre


def halo_of(proj_ref, i, lo, hi):
    start = pl.multiple_of(jnp.maximum(i * GROUP - 16, 0), 16)
    rows = proj_ref[pl.ds(start, 16), lo:hi].astype(F32)[16 - HALO :]
    return jnp.where(i > 0, rows, 0.0)


def peer_to(f, k, count):
    return lax.bitwise_xor(f, k) if count & (count - 1) == 0 else lax.rem(f + k, count)


def peer_from(f, k, count):
    if count & (count - 1) == 0:
        return lax.bitwise_xor(f, k)
    return lax.rem(f - k + count, count)


def spot(pair):
    me = lax.axis_index("seq")
    return me // pair, lax.rem(me, pair)


def assemble(pieces, whole_ref, chips, pair):
    tokens = whole_ref.shape[0] // (chips * pair)
    chip, core = spot(pair)
    for n, piece in enumerate(pieces):
        k, other = n % chips, n // chips
        at = lax.rem(chip - k + chips, chips) * pair + (1 - core if other else core)
        whole_ref[pl.ds(pl.multiple_of(at * tokens, tokens), tokens), :] = piece[...]


def columns_of(index, size):
    return pl.ds(pl.multiple_of(index * size, size), size)


def forward_kernel(heads, chips, pair, shards, *refs):
    pieces, refs = refs[: chips * pair], refs[chips * pair :]
    w_refs, refs = refs[:shards], refs[shards:]
    cw_ref, cb_ref, hp_ref, normed_ref, proj_ref, y_ref, core_ref, open_ref, state = refs
    width = heads * HEAD_DIM
    chans = width + 2 * STATE
    state[...] = jnp.zeros_like(state)
    depth = w_refs[0].shape[1]
    assemble(pieces, normed_ref, chips, pair)
    at = [peer_from(lax.axis_index("fsdp"), k, shards) for k in range(shards)]

    def step(i, _):
        rows = pl.ds(pl.multiple_of(i * GROUP, GROUP), GROUP)
        acc = dot(normed_ref[rows, columns_of(at[0], depth)], w_refs[0][...], 1, 1)
        for k in range(1, shards):
            acc = acc + dot(normed_ref[rows, columns_of(at[k], depth)], w_refs[k][...], 1, 1)
        proj = acc.astype(BF)
        proj_ref[rows, :] = proj
        v = proj[:, width : width + chans].astype(F32)
        taps = conv_taps(v, halo_of(proj_ref, i, width, width + chans))
        pre = conv_pre(taps, cw_ref[...], cb_ref[...])
        act = pre * jax.nn.sigmoid(pre)
        xs = act[:, :width]
        bs = act[:, width : width + STATE].astype(BF)
        cs = act[:, width + STATE :].astype(BF)
        dt = softplus(widen(proj[:, width + chans :].astype(F32)) + hp_ref[0:1])
        rate = -jnp.exp(hp_ref[1:2]) * dt
        run = pick_sums(tri(True).astype(F32).astype(BF), rate, 1, 0)
        run_t = run.T
        last = run[GROUP - 1 : GROUP]
        xdt = (xs * spread(dt, heads)).astype(BF)
        scores = dot(cs, bs, 1, 1)
        causal = tri(True)
        within = []
        for h in range(heads):
            gap = run[:, h : h + 1] - run_t[h : h + 1, :]
            decay = jnp.exp(jnp.where(causal, gap, -1e30))
            mixed = (scores * decay).astype(BF)
            within.append(dot(mixed, xdt[:, h * HEAD_DIM : (h + 1) * HEAD_DIM], 1, 0))
        memory = state[...]
        open_ref[i] = memory
        core = jnp.concatenate(within, axis=1) + spread(jnp.exp(run), heads) * dot(
            cs, memory.astype(BF), 1, 0
        )
        core_ref[rows, :] = core
        y_ref[rows, :] = (core + spread(hp_ref[2:3], heads) * xs).astype(BF)
        toward = (xdt.astype(F32) * spread(jnp.exp(last - run), heads)).astype(BF)
        state[...] = spread(jnp.exp(last), heads) * memory + dot(bs, toward, 0, 0)
        return 0

    lax.fori_loop(0, normed_ref.shape[0] // GROUP, step, 0, unroll=2)


def stats_kernel(chips, pair, *refs):
    pieces, refs = refs[: chips * pair], refs[chips * pair :]
    wo_refs, refs = refs[:chips], refs[chips:]
    y_ref, proj_ref, gain_ref, cot_ref, wo_ref, dg_ref, stats_ref = refs
    width = y_ref.shape[1]
    ones = jnp.ones((16, width), BF)
    assemble(pieces, cot_ref, chips, pair)
    part = wo_refs[0].shape[1]
    for k in range(chips):
        for core in range(pair):
            src = lax.rem(spot(pair)[0] - k + chips, chips) * pair + core
            wo_ref[pl.ds(pl.multiple_of(src * part, part), part), :] = wo_refs[k][core]

    def step(i, _):
        rows = pl.ds(pl.multiple_of(i * GROUP, GROUP), GROUP)
        dg = dot(cot_ref[rows, :], wo_ref[...], 1, 0)
        dg_ref[rows, :] = dg
        z = proj_ref[rows, :width].astype(F32)
        u = y_ref[rows, :].astype(F32) * (z * jax.nn.sigmoid(z))
        stats_ref[0:1, rows] = pick_sums(ones, u * u, 1, 1)[0:1]
        stats_ref[1:2, rows] = pick_sums(ones, u * gain_ref[...] * dg, 1, 1)[0:1]
        return 0

    lax.fori_loop(0, cot_ref.shape[0] // GROUP, step, 0, unroll=4)


def gate_kernel(
    inner,
    chips,
    pair,
    cot_ref,
    wo_ref,
    y_ref,
    proj_ref,
    gain_ref,
    dg_ref,
    stats_ref,
    *refs,
):
    out_refs, refs = refs[:pair], refs[pair:]
    gwo_refs, (dy_ref, dz_ref, ggain_ref, acc) = refs[:-4], refs[-4:]
    width = y_ref.shape[1]
    tokens = cot_ref.shape[0] // (chips * pair)
    part = wo_ref.shape[0] // (chips * pair)
    acc[...] = jnp.zeros_like(acc)
    ggain_ref[...] = jnp.zeros_like(ggain_ref)
    gain = gain_ref[...]
    chip, core = spot(pair)

    def device(k, other):
        return lax.rem(chip + k, chips) * pair + (1 - core if other else core)

    def step(k, _):
        for other in range(pair):
            rows = columns_of(device(k, other), tokens)
            st = jnp.concatenate([stats_ref[:, rows], jnp.zeros((6, tokens), F32)], axis=0).T
            r = lax.rsqrt(st[:, 0:1] / inner + EPS)
            y = y_ref[rows, :].astype(F32)
            z = proj_ref[rows, :width].astype(F32)
            sig = jax.nn.sigmoid(z)
            sz = z * sig
            u = y * sz
            dg = dg_ref[rows, :]
            ur = u * r
            gated = (ur * gain).astype(BF)
            du = r * (gain * dg) - u * (r * r * r * (st[:, 1:2] / inner))
            ggain_ref[...] += jnp.sum(dg * ur, axis=0, keepdims=True)
            dy_ref[rows, :] = (du * sz).astype(BF)
            dz_ref[rows, :] = (du * y * (sig * (1.0 + z * (1.0 - sig)))).astype(BF)
            out_refs[other][k, :tokens] = dot(gated, wo_ref[...], 1, 1).astype(BF)
            acc[...] += dot(cot_ref[rows, :], gated, 0, 0)
        return 0

    lax.fori_loop(0, chips, step, 0, unroll=2)
    for k in range(chips):
        for other in range(pair):
            piece = acc[columns_of(device(k, other), part), :].astype(BF)
            if gwo_refs:
                gwo_refs[other][k] = piece
                continue
            rows = out_refs[other].shape[1] - tokens
            for j in range(part // rows):
                lanes = slice(j * width, (j + 1) * width)
                out_refs[other][k, tokens:, lanes] = piece[j * rows : (j + 1) * rows]


def backward_kernel(
    heads,
    chips,
    pair,
    shards,
    proj_ref,
    core_ref,
    open_ref,
    dy_ref,
    dz_ref,
    cw_ref,
    cb_ref,
    hp_ref,
    *refs,
):
    w_refs, refs = refs[:shards], refs[shards:]
    dn_refs, refs = refs[:pair], refs[pair:]
    dproj_ref, gcw_ref, gcb_ref, ghp_ref, dstate, ahead = refs
    shard = w_refs[0].shape[1]
    tokens = proj_ref.shape[0] // (chips * pair)
    per = tokens // GROUP
    at = [peer_from(lax.axis_index("fsdp"), k, shards) for k in range(shards)]
    chip, core = spot(pair)
    width = heads * HEAD_DIM
    chans = width + 2 * STATE
    blocks = proj_ref.shape[0] // GROUP
    dstate[...] = jnp.zeros_like(dstate)
    ahead[...] = jnp.zeros_like(ahead)
    gcw_ref[...] = jnp.zeros_like(gcw_ref)
    gcb_ref[...] = jnp.zeros_like(gcb_ref)
    ghp_ref[...] = jnp.zeros_like(ghp_ref)
    fold = (
        lax.broadcasted_iota(jnp.int32, (width, LANES), 0) // HEAD_DIM
        == lax.broadcasted_iota(jnp.int32, (width, LANES), 1)
    ).astype(F32).astype(BF)

    def step(n, _):
        i = blocks - 1 - n
        rows = pl.ds(pl.multiple_of(i * GROUP, GROUP), GROUP)
        v = proj_ref[rows, width : width + chans].astype(F32)
        taps = conv_taps(v, halo_of(proj_ref, i, width, width + chans))
        cw = cw_ref[...]
        pre = conv_pre(taps, cw, cb_ref[...])
        sig = jax.nn.sigmoid(pre)
        act = pre * sig
        xs = act[:, :width]
        bs = act[:, width : width + STATE].astype(BF)
        cs = act[:, width + STATE :].astype(BF)
        shifted = widen(proj_ref[rows, width + chans :].astype(F32)) + hp_ref[0:1]
        dt = softplus(shifted)
        neg = -jnp.exp(hp_ref[1:2])
        rate = neg * dt
        run = pick_sums(tri(True).astype(F32).astype(BF), rate, 1, 0)
        run_t = run.T
        last = run[GROUP - 1 : GROUP]
        dt_x = spread(dt, heads)
        xdt = (xs * dt_x).astype(BF)
        scores = dot(cs, bs, 1, 1)
        causal = tri(True)
        dyb = dy_ref[rows, :]
        dy = dyb.astype(F32)
        dscores = jnp.zeros((GROUP, GROUP), F32)
        parts = []
        for h in range(heads):
            cols = slice(h * HEAD_DIM, (h + 1) * HEAD_DIM)
            gap = run[:, h : h + 1] - run_t[h : h + 1, :]
            decay = jnp.exp(jnp.where(causal, gap, -1e30))
            mixed = (scores * decay).astype(BF)
            parts.append(dot(mixed, dyb[:, cols], 0, 0))
            dscores = dscores + dot(dyb[:, cols], xdt[:, cols], 1, 1) * decay
        dscores = dscores.astype(BF)
        memory = open_ref[i]
        mem_b = memory.astype(BF)
        ds = dstate[...]
        ds_b = ds.astype(BF)
        edy = (spread(jnp.exp(run), heads) * dy).astype(BF)
        dec = spread(jnp.exp(last - run), heads)
        xdt_f = xdt.astype(F32)
        inflow = dec * dot(bs, ds_b, 1, 0)
        dxdt = jnp.concatenate(parts, axis=1) + inflow
        dc = dot(dscores, bs, 1, 0) + dot(edy, mem_b, 1, 1)
        db = dot(dscores, cs, 0, 0) + dot((xdt_f * dec).astype(BF), ds_b, 1, 1)
        carried = spread(jnp.exp(last), heads)
        dstate[...] = dot(cs, edy, 0, 0) + carried * ds
        dx = dt_x * dxdt + spread(hp_ref[2:3], heads) * dy
        tops = jnp.concatenate(
            [
                jnp.sum(xdt_f * inflow, axis=0, keepdims=True)
                + carried * jnp.sum(ds * memory, axis=0, keepdims=True),
                jnp.sum(dy * xs, axis=0, keepdims=True),
                jnp.zeros((6, width), F32),
            ],
            axis=0,
        )
        folded = pick_sums(
            fold,
            jnp.concatenate([xs * dxdt, dy * core_ref[rows, :] - xdt_f * dxdt, tops], axis=0),
            0,
            1,
            first=False,
        )
        dend = folded[2 * GROUP : 2 * GROUP + 1]
        drate = pick_sums(tri(False).astype(F32).astype(BF), folded[GROUP : 2 * GROUP], 1, 0) + dend
        ddt = folded[:GROUP] + neg * drate
        ddtr = ddt * jax.nn.sigmoid(shifted)
        ghp_ref[0:1] += jnp.sum(ddtr, axis=0, keepdims=True)
        ghp_ref[1:2] += jnp.sum(drate * rate, axis=0, keepdims=True)
        ghp_ref[2:3] += folded[2 * GROUP + 1 : 2 * GROUP + 2]
        dact = jnp.concatenate([dx, db, dc], axis=1)
        dpre = dact * (sig * (1.0 + pre * (1.0 - sig)))
        gcb_ref[...] += jnp.sum(dpre, axis=0, keepdims=True)
        for k in range(CONV_W):
            gcw_ref[k : k + 1] += jnp.sum(dpre * taps[k], axis=0, keepdims=True)
        ext = jnp.concatenate([dpre, ahead[...]], axis=0)
        ahead[...] = dpre[:HALO]
        dv = cw[CONV_W - 1 :] * dpre
        for k in range(CONV_W - 1):
            moved = pltpu.roll(ext, ext.shape[0] - (CONV_W - 1 - k), 0)[:GROUP]
            dv = dv + cw[k : k + 1] * moved
        few = dproj_ref.shape[1] - width - chans
        dproj = jnp.concatenate(
            [dz_ref[rows, :], dv.astype(BF), ddtr[:, :few].astype(BF)], axis=1
        )
        dproj_ref[rows, :] = dproj
        owner = i // per
        k = lax.rem(owner // pair - chip + chips, chips)
        inside = pl.ds(pl.multiple_of((i % per) * GROUP, GROUP), GROUP)
        dn = [dot(dproj, w[...], 1, 0).astype(BF) for w in w_refs]
        for other in range(pair):

            @pl.when((owner % pair != core) == bool(other))
            def _():
                for j in range(shards):
                    dn_refs[other][k, inside, columns_of(at[j], shard)] = dn[j]

        return 0

    lax.fori_loop(0, blocks, step, 0, unroll=2)


def columns_kernel(heads, shards, dproj_ref, normed_ref, *refs):
    w_refs, refs = refs[:shards], refs[shards:]
    gcw_ref, gcb_ref, ghp_ref, ggain_ref, refs = *refs[:4], refs[4:]
    g_refs, (gnorm_ref, slots_ref, common_ref) = refs[:shards], refs[shards:]
    width = ggain_ref.shape[1]
    lanes = min(width, LANES)
    packed = ghp_ref[0:1]
    for n in range(1, 3):
        packed = packed + pltpu.roll(ghp_ref[n : n + 1], n * heads, 1)
    packed = packed[:, :lanes]
    if lanes < width:
        packed = jnp.concatenate([packed, jnp.zeros((1, width - lanes), F32)], axis=1)
    slots_ref[...] = jnp.zeros_like(slots_ref)
    slot = jnp.concatenate(
        [
            gcw_ref[:, :width],
            gcb_ref[:, :width],
            ggain_ref[...],
            packed,
            jnp.zeros((1, width), F32),
        ],
        axis=0,
    )
    for j in range(width // lanes):
        slots_ref[lax.axis_index("seq"), j] = slot[:, j * lanes : (j + 1) * lanes]
    for j in range(2 * STATE // LANES):
        at = slice(width + j * LANES, width + (j + 1) * LANES)
        common_ref[j] = jnp.concatenate(
            [gcw_ref[:, at], gcb_ref[:, at], jnp.zeros((3, LANES), F32)], axis=0
        )
    shard = w_refs[0].shape[1]
    for k in range(shards):
        at = columns_of(peer_to(lax.axis_index("fsdp"), k, shards), shard)
        g = dot(dproj_ref[...], normed_ref[:, at], 0, 0)
        g_refs[k][...] = g.astype(BF)
        source = peer_index(k, shards)
        gnorm_ref[0:1, at] = jnp.sum(g * w_refs[source][...].astype(F32), axis=0, keepdims=True)


def chosen(index, start, size):
    row = lax.broadcasted_iota(jnp.int32, (size, index.shape[1]), 0) + start
    return (row == index).astype(F32).astype(BF)


def table_row(table_ref):
    return table_ref[pl.ds(lax.axis_index("seq"), 1), :]


def pick_kernel(table_ref, w_ref, *out_refs):
    index, start = table_row(table_ref), 0
    for out_ref in out_refs:
        items = index[:, start : start + out_ref.shape[0]]
        out_ref[...] = dot(chosen(items, 0, w_ref.shape[0]), w_ref[...], 0, 0).astype(BF)
        start += out_ref.shape[0]


def place_kernel(split, kinds, table_ref, w_ref, *refs):
    arrived, out_ref = refs[:-1], refs[-1]
    index = table_row(table_ref)
    for rows, kind in ((slice(0, split), False), (slice(split, out_ref.shape[0]), True)):
        start = w_ref.shape[0]
        out = dot(chosen(index[:, rows], 0, start), w_ref[...], 0, 0)
        for shared, piece in zip(kinds, arrived):
            if shared == kind:
                out = out + dot(chosen(index[:, rows], start, piece.shape[0]), piece[...], 0, 0)
            start += piece.shape[0]
        out_ref[rows, :] = out.astype(BF)


def back_kernel(kinds, table_ref, g_ref, common_ref, pool_ref, *out_refs):
    split = pool_ref.shape[0] - common_ref.shape[0]
    pool_ref[:split] = g_ref[:split]
    pool_ref[split:] = common_ref[...]
    index, start = table_row(table_ref), 0
    for shared, out_ref in zip(kinds, out_refs):
        items = index[:, start : start + out_ref.shape[0]]
        if shared:
            out = dot(chosen(items, split, common_ref.shape[0]), common_ref[...], 0, 0)
        else:
            out = dot(chosen(items, 0, split), g_ref[:split], 0, 0)
        out_ref[...] = out.astype(BF)
        start += out_ref.shape[0]


def home_kernel(table_ref, *refs):
    pieces, out_ref = refs[:-1], refs[-1]
    index, start, out = table_row(table_ref), 0, None
    for piece in pieces:
        items = index[:, start : start + piece.shape[0]]
        part = dot(chosen(items, 0, out_ref.shape[0]), piece[...], 1, 0)
        out = part if out is None else out + part
        start += piece.shape[0]
    out_ref[...] = out


def hold_kernel(tokens, keep_ref, got_ref, own_ref, *out_refs):
    rows = keep_ref.shape[1]
    for k in range(keep_ref.shape[0]):
        total = keep_ref[k, :tokens].astype(F32) + got_ref[k, :tokens].astype(F32)
        if k == 0:
            own_ref[:tokens] = total
        else:
            out_refs[k - 1][:tokens] = total.astype(BF)
        if rows > tokens:
            extra = rows - tokens
            for n, ref in enumerate((keep_ref, got_ref)):
                at = slice(tokens + n * extra, tokens + (n + 1) * extra)
                if k == 0:
                    own_ref[at] = ref[k, tokens:].astype(F32)
                else:
                    out_refs[k - 1][at] = ref[k, tokens:]


def peer_index(k, count):
    return k if count & (count - 1) == 0 else (count - k) % count


def call(kernel, outs, scratch, *args):
    whole = pl.BlockSpec(memory_space=pltpu.VMEM)
    return pl.pallas_call(
        kernel,
        out_shape=[jax.ShapeDtypeStruct(shape, kind) for shape, kind in outs],
        in_specs=[whole] * len(args),
        out_specs=[whole] * len(outs),
        scratch_shapes=[pltpu.VMEM(shape, kind) for shape, kind in scratch],
    )(*args)


def per_device(
    fsdp,
    seq,
    block_input,
    norm_gain,
    w_in,
    conv_w,
    conv_b,
    dt_bias,
    a_log,
    skip_gain,
    gate_gain,
    w_out,
    out_cotangent,
):
    links = Links(fsdp, seq)
    residual = block_input[0]
    grad_out = out_cotangent[0]
    tokens, depth = residual.shape
    length = tokens * seq
    heads_all = dt_bias.shape[0]
    inner = gate_gain.shape[0]
    heads = heads_all // seq
    width = inner // seq
    chans = width + 2 * STATE
    routes = Routes(seq, w_in.shape[1] * seq, inner, STATE, heads_all)
    me = links.s
    shared = routes.shared

    mean = jnp.mean(residual * residual, axis=-1, keepdims=True)
    scale = lax.rsqrt(mean + EPS)
    normed_half = (residual * scale * norm_gain).astype(BF)

    w_cols = w_in.T
    rows_here = w_in.shape[0]
    picked = call(
        pick_kernel,
        [((size, rows_here), BF) for size in routes.sizes],
        [],
        jnp.asarray(routes.send),
        w_cols,
    )
    arrived = []
    for r, group in enumerate(routes.rounds):
        arrived.append(lax.ppermute(picked[r], "seq", [(p[0], p[1]) for p in group]))
    (mine,) = call(
        functools.partial(place_kernel, 2 * width, routes.kinds),
        [((routes.rows, rows_here), BF)],
        [],
        jnp.asarray(routes.take),
        w_cols,
        *arrived,
    )
    common = mine[2 * width :]
    if links.pair == 2:
        common = common + lax.ppermute(
            common, "seq", [(i, i - 1) for i in range(1, seq, 2)]
        )
    head_row = jnp.arange(ceil_to(heads, 16), dtype=jnp.int32)
    head_row = jnp.where(head_row < heads, 2 * STATE + me * heads + head_row, -1)
    head_pick = one_hot(head_row, shared)
    w_mine = jnp.concatenate(
        [mine[: 2 * width], common[: 2 * STATE], dot(head_pick, common, 1, 0).astype(BF)], axis=0
    )
    normed = links.gather_seq(normed_half)
    w_all = links.gather_fsdp(w_mine)

    wo_half = w_out.reshape(-1, width, w_out.shape[1]).transpose(0, 2, 1)
    wo_rows = jnp.zeros((fsdp,) + wo_half.shape, BF)
    for k, piece in enumerate(links.gather_fsdp(wo_half)):
        wo_rows = lax.dynamic_update_index_in_dim(wo_rows, piece, peer_from(links.f, k, fsdp), 0)
    wo_rows = wo_rows.reshape((links.chips, links.pair) + wo_half.shape[1:])
    order = [links.chip_at(k) for k in range(links.chips)]

    def parity(core):
        picks = [lax.dynamic_slice(wo_rows, (c, core, 0, 0), (1, 1) + wo_half.shape[1:]) for c in order]
        return jnp.concatenate(picks, axis=0)[:, 0]

    wo = links.exchange_seq(parity(links.core), parity(1 - links.core))
    cot_half = grad_out.astype(BF)
    cot = links.gather_seq(cot_half)

    def local(vector, size, start):
        return lax.dynamic_slice_in_dim(vector, start, size, vector.ndim - 1)

    cw = jnp.concatenate([local(conv_w[:, :inner], width, me * width), conv_w[:, inner:]], axis=1)
    cb = jnp.concatenate([local(conv_b[:inner], width, me * width), conv_b[inner:]])[None]
    per_head = jnp.stack([local(p, heads, me * heads) for p in (dt_bias, a_log, skip_gain)])
    hp = jnp.pad(per_head, ((0, 5), (0, LANES - heads)))
    gain = local(gate_gain, width, me * width)[None]
    narrow = ceil_to(heads, 16)
    cols = 2 * width + 2 * STATE + narrow
    blocks = length // GROUP

    chips, pair = links.chips, links.pair
    normed_all, proj, y, core, opened = call(
        functools.partial(forward_kernel, heads, chips, pair, fsdp),
        [
            ((length, depth), BF),
            ((length, cols), BF),
            ((length, width), BF),
            ((length, width), F32),
            ((blocks, STATE, width), F32),
        ],
        [((STATE, width), F32)],
        *normed,
        *w_all,
        cw,
        cb,
        hp,
    )
    cot_all, wo_all, dgated, stats = call(
        functools.partial(stats_kernel, chips, pair),
        [((length, depth), BF), ((depth, width), BF), ((length, width), F32), ((2, length), F32)],
        [],
        *cot,
        *wo,
        y,
        proj,
        gain,
    )
    stats = links.sum_seq(stats)
    halves = [((chips, tokens, depth), BF)] * pair
    part = depth // seq
    extra = part * width // depth
    together = pair == 2 and extra % 16 == 0 and width % LANES == 0
    out_halves = [((chips, tokens + extra, depth), BF)] * pair if together else halves
    quarters = [] if together else [((chips, part, width), BF)] * pair
    gate_outs = call(
        functools.partial(gate_kernel, float(inner), chips, pair),
        out_halves
        + quarters
        + [((length, width), BF), ((length, width), BF), ((1, width), F32)],
        [((depth, width), F32)],
        cot_all,
        wo_all,
        y,
        proj,
        gain,
        dgated,
        stats,
    )
    out_halves, gwo_halves = gate_outs[:pair], gate_outs[pair:-3]
    dy, dz, ggain = gate_outs[-3:]
    back_outs = call(
        functools.partial(backward_kernel, heads, chips, pair, fsdp),
        halves
        + [((length, cols), BF), ((CONV_W, chans), F32), ((1, chans), F32), ((8, LANES), F32)],
        [((STATE, width), F32), ((HALO, chans), F32)],
        proj,
        core,
        opened,
        dy,
        dz,
        cw,
        cb,
        hp,
        *w_all,
    )
    dn_halves = back_outs[:pair]
    dproj, gcw, gcb, ghp = back_outs[pair:]
    shard = depth // fsdp
    lanes = min(width, LANES)
    *g_cols, g_norm, slots, g_shared = call(
        functools.partial(columns_kernel, heads, fsdp),
        [((cols, shard), BF)] * fsdp
        + [
            ((1, depth), F32),
            ((seq, width // lanes, 8, lanes), F32),
            ((2 * STATE // LANES, 8, LANES), F32),
        ],
        [],
        dproj,
        normed_all,
        *w_all,
        gcw,
        gcb,
        ghp,
        ggain,
    )

    out_sum, arrived = links.scatter_seq(out_halves[0], out_halves[-1], tokens)
    block_out = residual + out_sum
    if together:
        gwo = []
        for piece in arrived:
            both = piece[tokens:].astype(BF).reshape(2, extra, part // extra, width)
            both = both.transpose(0, 2, 1, 3).reshape(2, part, width)
            gwo.append(jnp.where(links.core == 0, both, both[::-1]))
    else:
        gwo = links.exchange_seq(gwo_halves[0], gwo_halves[-1])
    gwo_rows = jnp.zeros((chips,) + gwo[0].shape, BF)
    for k, piece in enumerate(gwo):
        gwo_rows = lax.dynamic_update_index_in_dim(gwo_rows, piece, links.chip_at(-k), 0)
    gwo_rows = gwo_rows.reshape((fsdp, seq // fsdp, depth // seq, width))
    to = [
        lax.dynamic_index_in_dim(gwo_rows, peer_to(links.f, k, fsdp), 0, keepdims=False)
        for k in range(fsdp)
    ]
    owned_w_out = links.scatter_fsdp(to).transpose(0, 2, 1).reshape(w_out.shape)

    g_mine = links.scatter_fsdp(g_cols)
    dnormed, _ = links.scatter_seq(dn_halves[0], dn_halves[-1], tokens)
    dscaled = dnormed * norm_gain
    du_norm = scale * dscaled - residual * (
        scale * scale * scale * jnp.mean(residual * dscaled, axis=-1, keepdims=True)
    )
    grad_in = grad_out + du_norm

    g_half = g_mine.astype(BF)
    g_heads = dot(head_pick, g_half[2 * width + 2 * STATE :], 0, 0)[2 * STATE :]
    g_common = jnp.concatenate([g_half[2 * width : 2 * width + 2 * STATE], g_heads.astype(BF)])
    if links.pair == 2:
        other = lax.ppermute(g_common, "seq", [(i, i + 1) for i in range(0, seq, 2)])
        g_common = (g_common.astype(F32) + other.astype(F32)).astype(BF)
    g_pool, *sent = call(
        functools.partial(back_kernel, routes.kinds),
        [((routes.rows, rows_here), BF)] + [((size, rows_here), BF) for size in routes.sizes],
        [],
        jnp.asarray(routes.back),
        g_half,
        g_common,
    )
    homed = []
    for r, group in enumerate(routes.rounds):
        homed.append(lax.ppermute(sent[r], "seq", [(p[1], p[0]) for p in group]))
    (owned_w_in,) = call(
        home_kernel, [(w_cols.shape, F32)], [], jnp.asarray(routes.home), g_pool, *homed
    )
    owned_w_in = owned_w_in.T

    pieces, _ = lax.optimization_barrier(([slots, g_shared, g_norm], tuple(g_cols)))
    packed = jnp.concatenate([p.reshape(-1, LANES) for p in pieces], axis=0)
    packed = links.sum_fsdp(links.sum_seq(packed))
    first = slots.size // LANES
    slots = packed[:first].reshape(slots.shape)
    second = first + g_shared.size // LANES
    g_shared = packed[first:second].reshape(g_shared.shape)
    g_norm = packed[second:].reshape(-1) / norm_gain
    slots = slots.transpose(0, 2, 1, 3).reshape(seq, 8, width)
    g_shared = g_shared.transpose(1, 0, 2).reshape(8, 2 * STATE)
    g_conv_w = jnp.concatenate(
        [slots[:, :CONV_W].transpose(1, 0, 2).reshape(CONV_W, inner), g_shared[:CONV_W]], axis=1
    )
    g_conv_b = jnp.concatenate([slots[:, CONV_W].reshape(inner), g_shared[CONV_W]])
    g_gain = slots[:, CONV_W + 1].reshape(inner)
    g_head = [slots[:, CONV_W + 2, n * heads : (n + 1) * heads].reshape(-1) for n in range(3)]
    return (
        block_out[None],
        grad_in[None],
        g_norm,
        owned_w_in,
        g_conv_w,
        g_conv_b,
        *g_head,
        g_gain,
        owned_w_out,
    )


def solution(mesh):
    weights = P("fsdp", "seq")
    acts = P("fsdp", "seq", None)
    fsdp, seq = mesh.shape["fsdp"], mesh.shape["seq"]

    def body(*args):
        return per_device(fsdp, seq, *args)

    return jax.shard_map(
        body,
        mesh=mesh,
        in_specs=(acts, P(), weights, P(), P(), P(), P(), P(), P(), weights, acts),
        out_specs=(acts, acts, P(), weights, P(), P(), P(), P(), P(), P(), weights),
        check_vma=False,
    )
```

```python
import functools

import jax
import jax.numpy as jnp
import numpy as np
from jax import lax
from jax.experimental import pallas as pl
from jax.experimental.pallas import tpu as pltpu
from jax.sharding import PartitionSpec as P


HEAD_DIM = 64
STATE = 128
CONV_W = 4
GROUP = 128
LANES = 128
EPS = 1e-05
HALO = 8
BF = jnp.bfloat16
F32 = jnp.float32


def ceil_to(n, k):
    return (n + k - 1) // k * k


def dot(a, b, ca, cb):
    return lax.dot_general(a, b, (((ca,), (cb,)), ((), ())), preferred_element_type=F32)


def thirds(x):
    parts = []
    for _ in range(3):
        part = x.astype(BF)
        parts.append(part)
        x = x - part.astype(F32)
    return parts


def pick_sums(picks, x, cp, cx, first=True):
    if first:
        return sum(dot(picks, part, cp, cx) for part in thirds(x))
    return sum(dot(part, picks, cx, cp) for part in thirds(x))


class Routes:
    def __init__(self, seq, columns, inner, state, heads, merged=False):
        self.pair = 2 if seq % 2 == 0 else 1
        self.own = columns // seq
        self.width = inner // seq
        self.shared = 2 * state + heads
        width, own, pair = self.width, self.own, self.pair
        pieces = []
        for dst in range(seq):
            wants = [(dst * width, width, 0), (inner + dst * width, width, width)]
            if dst % pair == pair - 1:
                wants.append((2 * inner, self.shared, 2 * width))
            for start, length, at in wants:
                col = start
                while col < start + length:
                    src = col // own
                    stop = min(start + length, (src + 1) * own)
                    pieces.append((src, dst, col - src * own, stop - col, at + col - start))
                    col = stop
        self.local = [p for p in pieces if p[0] == p[1]]
        remote = [p for p in pieces if p[0] != p[1]]
        common = [p for p in remote if p[4] >= 2 * width]
        if merged:
            self.rounds = self.color(remote)
            self.kinds = [None] * len(self.rounds)
        else:
            self.rounds = self.color(common) + self.color([p for p in remote if p[4] < 2 * width])
            self.kinds = [group[0][4] >= 2 * width for group in self.rounds]
        self.sizes = [ceil_to(max(p[3] for p in group), 16) for group in self.rounds]
        self.starts = [sum(self.sizes[:r]) for r in range(len(self.sizes))]
        total = sum(self.sizes)
        self.rows = 2 * width + self.shared
        self.send = np.full((seq, total), -1, np.int32)
        self.take = np.full((seq, self.rows), -1, np.int32)
        self.back = np.full((seq, total), -1, np.int32)
        self.home = np.full((seq, self.rows + total), -1, np.int32)
        for src, dst, at, length, to in self.local:
            for i in range(length):
                self.take[dst, to + i] = at + i
                self.home[dst, to + i] = at + i
        for r, group in enumerate(self.rounds):
            for src, dst, at, length, to in group:
                first = self.starts[r]
                for i in range(length):
                    self.send[src, first + i] = at + i
                    self.take[dst, to + i] = own + first + i
                    self.back[dst, first + i] = to + i
                    self.home[src, self.rows + first + i] = at + i

    @staticmethod
    def color(pieces):
        rounds = []
        left = sorted(pieces, key=lambda p: -p[3])
        degree = {}
        for p in left:
            degree[("s", p[0])] = degree.get(("s", p[0]), 0) + 1
            degree[("d", p[1])] = degree.get(("d", p[1]), 0) + 1
        limit = max(degree.values()) if degree else 0
        used = {}
        colors = {}

        def free(node):
            taken = used.setdefault(node, {})
            return next(c for c in range(limit) if c not in taken)

        for index, p in enumerate(left):
            u, v = ("s", p[0]), ("d", p[1])
            a, b = free(u), free(v)
            if a != b and a in used[v]:
                path, node, want = [], v, a
                while want in used[node]:
                    edge = used[node][want]
                    path.append(edge)
                    q = left[edge]
                    ends = (("s", q[0]), ("d", q[1]))
                    node = ends[1] if node == ends[0] else ends[0]
                    want = b if want == a else a
                for edge in path:
                    q = left[edge]
                    for end in (("s", q[0]), ("d", q[1])):
                        used[end].pop(colors[edge], None)
                for edge in path:
                    q = left[edge]
                    colors[edge] = b if colors[edge] == a else a
                    for end in (("s", q[0]), ("d", q[1])):
                        used[end][colors[edge]] = edge
            colors[index] = a
            used[u][a] = index
            used[v][a] = index
        for c in range(limit):
            rounds.append([left[i] for i in range(len(left)) if colors[i] == c])
        return rounds


def one_hot(index, size):
    return (index[:, None] == lax.broadcasted_iota(jnp.int32, (index.shape[0], size), 1)).astype(BF)


class Links:
    def __init__(self, fsdp, seq):
        self.F, self.S = fsdp, seq
        self.pair = 2 if seq % 2 == 0 else 1
        self.chips = seq // self.pair
        self.f = lax.axis_index("fsdp")
        self.s = lax.axis_index("seq")
        self.chip = self.s // self.pair
        self.core = self.s % self.pair

    def swap(self, x):
        return lax.ppermute(x, "seq", [(i, i ^ 1) for i in range(self.S)])

    def hop(self, x, k):
        step = self.pair * k
        return lax.ppermute(x, "seq", [(i, (i + step) % self.S) for i in range(self.S)])

    def chip_at(self, k):
        return lax.rem(self.chip + k + self.chips, self.chips)

    def across(self, x, k):
        if self.F & (self.F - 1) == 0:
            pairs = [(i, i ^ k) for i in range(self.F)]
        else:
            pairs = [(i, (i + k) % self.F) for i in range(self.F)]
        return lax.ppermute(x, "fsdp", pairs)

    def gather_seq(self, x):
        mine, other = [x], []
        for k in range(1, self.chips):
            mine.append(self.hop(x, k))
        if self.pair == 2:
            for k in range(self.chips):
                other.append(self.swap(mine[k]))
        return mine + other

    def scatter_seq(self, keep, give, tokens):
        chips, rows, depth = keep.shape
        rows += rows - tokens
        if self.pair == 2:
            got = self.swap(give)
            own, *held = call(
                functools.partial(hold_kernel, tokens),
                [((rows, depth), F32)] + [((rows, depth), BF)] * (chips - 1),
                [],
                keep,
                got,
            )
        else:
            own, held = keep[0].astype(F32), [keep[k] for k in range(1, chips)]
        arrived = [own]
        for k in range(1, chips):
            arrived.append(self.hop(held[k - 1], k))
        return sum((a[:tokens].astype(F32) for a in arrived[1:]), own[:tokens]), arrived

    def exchange_seq(self, keep, give):
        if self.pair == 2:
            got = self.swap(give)
            first = self.core == 0
            parts = jnp.stack([jnp.where(first, keep, got), jnp.where(first, got, keep)], 1)
        else:
            parts = keep[:, None]
        out = [parts[0]]
        for k in range(1, self.chips):
            out.append(self.hop(parts[k], k))
        return out

    def gather_fsdp(self, x):
        out = [x]
        for k in range(1, self.F):
            out.append(self.across(x, k))
        return out

    def scatter_fsdp(self, parts):
        total = parts[0].astype(F32)
        for k in range(1, self.F):
            total = total + self.across(parts[k], k).astype(F32)
        return total

    def sum_seq(self, x):
        if self.pair == 2:
            x = x + self.swap(x)
        total = x
        for k in range(1, self.chips):
            total = total + self.hop(x, k)
        return total

    def sum_fsdp(self, x):
        total = x
        for k in range(1, self.F):
            total = total + self.across(x, k)
        return total


def spread(values, heads):
    rows = values.shape[0]
    return jnp.concatenate(
        [jnp.broadcast_to(values[:, h : h + 1], (rows, HEAD_DIM)) for h in range(heads)], axis=1
    )


def widen(x):
    return jnp.concatenate([x, jnp.zeros((x.shape[0], LANES - x.shape[1]), x.dtype)], axis=1)


def softplus(x):
    return jnp.maximum(x, 0.0) + jnp.log1p(jnp.exp(-jnp.abs(x)))


def tri(lower):
    row = lax.broadcasted_iota(jnp.int32, (GROUP, GROUP), 0)
    col = lax.broadcasted_iota(jnp.int32, (GROUP, GROUP), 1)
    return (row >= col) if lower else (row <= col)


def conv_taps(v, halo):
    ext = jnp.concatenate([halo, v], axis=0)
    return [
        (pltpu.roll(ext, CONV_W - 1 - k, 0) if k < CONV_W - 1 else ext)[HALO:]
        for k in range(CONV_W)
    ]


def conv_pre(taps, cw, cb):
    pre = cb + cw[0:1] * taps[0]
    for k in range(1, CONV_W):
        pre = pre + cw[k : k + 1] * taps[k]
    return pre


def halo_of(proj_ref, i, lo, hi):
    start = pl.multiple_of(jnp.maximum(i * GROUP - 16, 0), 16)
    rows = proj_ref[pl.ds(start, 16), lo:hi].astype(F32)[16 - HALO :]
    return jnp.where(i > 0, rows, 0.0)


def peer_to(f, k, count):
    return lax.bitwise_xor(f, k) if count & (count - 1) == 0 else lax.rem(f + k, count)


def peer_from(f, k, count):
    if count & (count - 1) == 0:
        return lax.bitwise_xor(f, k)
    return lax.rem(f - k + count, count)


def spot(pair):
    me = lax.axis_index("seq")
    return me // pair, lax.rem(me, pair)


def assemble(pieces, whole_ref, chips, pair):
    tokens = whole_ref.shape[0] // (chips * pair)
    chip, core = spot(pair)
    for n, piece in enumerate(pieces):
        k, other = n % chips, n // chips
        at = lax.rem(chip - k + chips, chips) * pair + (1 - core if other else core)
        whole_ref[pl.ds(pl.multiple_of(at * tokens, tokens), tokens), :] = piece[...]


def columns_of(index, size):
    return pl.ds(pl.multiple_of(index * size, size), size)


def forward_kernel(heads, chips, pair, shards, *refs):
    pieces, refs = refs[: chips * pair], refs[chips * pair :]
    w_refs, refs = refs[:shards], refs[shards:]
    cw_ref, cb_ref, hp_ref, normed_ref, proj_ref, y_ref, core_ref, open_ref, state = refs
    width = heads * HEAD_DIM
    chans = width + 2 * STATE
    state[...] = jnp.zeros_like(state)
    depth = w_refs[0].shape[1]
    assemble(pieces, normed_ref, chips, pair)
    at = [peer_from(lax.axis_index("fsdp"), k, shards) for k in range(shards)]

    def step(i, _):
        rows = pl.ds(pl.multiple_of(i * GROUP, GROUP), GROUP)
        acc = dot(normed_ref[rows, columns_of(at[0], depth)], w_refs[0][...], 1, 1)
        for k in range(1, shards):
            acc = acc + dot(normed_ref[rows, columns_of(at[k], depth)], w_refs[k][...], 1, 1)
        proj = acc.astype(BF)
        proj_ref[rows, :] = proj
        v = proj[:, width : width + chans].astype(F32)
        taps = conv_taps(v, halo_of(proj_ref, i, width, width + chans))
        pre = conv_pre(taps, cw_ref[...], cb_ref[...])
        act = pre * jax.nn.sigmoid(pre)
        xs = act[:, :width]
        bs = act[:, width : width + STATE].astype(BF)
        cs = act[:, width + STATE :].astype(BF)
        dt = softplus(widen(proj[:, width + chans :].astype(F32)) + hp_ref[0:1])
        rate = -jnp.exp(hp_ref[1:2]) * dt
        run = pick_sums(tri(True).astype(F32).astype(BF), rate, 1, 0)
        run_t = run.T
        last = run[GROUP - 1 : GROUP]
        xdt = (xs * spread(dt, heads)).astype(BF)
        scores = dot(cs, bs, 1, 1)
        causal = tri(True)
        within = []
        for h in range(heads):
            gap = run[:, h : h + 1] - run_t[h : h + 1, :]
            decay = jnp.exp(jnp.where(causal, gap, -1e30))
            mixed = (scores * decay).astype(BF)
            within.append(dot(mixed, xdt[:, h * HEAD_DIM : (h + 1) * HEAD_DIM], 1, 0))
        memory = state[...]
        open_ref[i] = memory
        core = jnp.concatenate(within, axis=1) + spread(jnp.exp(run), heads) * dot(
            cs, memory.astype(BF), 1, 0
        )
        core_ref[rows, :] = core
        y_ref[rows, :] = (core + spread(hp_ref[2:3], heads) * xs).astype(BF)
        toward = (xdt.astype(F32) * spread(jnp.exp(last - run), heads)).astype(BF)
        state[...] = spread(jnp.exp(last), heads) * memory + dot(bs, toward, 0, 0)
        return 0

    lax.fori_loop(0, normed_ref.shape[0] // GROUP, step, 0, unroll=2)


def stats_kernel(chips, pair, *refs):
    pieces, refs = refs[: chips * pair], refs[chips * pair :]
    wo_refs, refs = refs[:chips], refs[chips:]
    y_ref, proj_ref, gain_ref, cot_ref, wo_ref, dg_ref, stats_ref = refs
    width = y_ref.shape[1]
    ones = jnp.ones((16, width), BF)
    assemble(pieces, cot_ref, chips, pair)
    part = wo_refs[0].shape[1]
    for k in range(chips):
        for core in range(pair):
            src = lax.rem(spot(pair)[0] - k + chips, chips) * pair + core
            wo_ref[pl.ds(pl.multiple_of(src * part, part), part), :] = wo_refs[k][core]

    def step(i, _):
        rows = pl.ds(pl.multiple_of(i * GROUP, GROUP), GROUP)
        dg = dot(cot_ref[rows, :], wo_ref[...], 1, 0)
        dg_ref[rows, :] = dg
        z = proj_ref[rows, :width].astype(F32)
        u = y_ref[rows, :].astype(F32) * (z * jax.nn.sigmoid(z))
        stats_ref[0:1, rows] = pick_sums(ones, u * u, 1, 1)[0:1]
        stats_ref[1:2, rows] = pick_sums(ones, u * gain_ref[...] * dg, 1, 1)[0:1]
        return 0

    lax.fori_loop(0, cot_ref.shape[0] // GROUP, step, 0, unroll=4)


def gate_kernel(
    inner,
    chips,
    pair,
    cot_ref,
    wo_ref,
    y_ref,
    proj_ref,
    gain_ref,
    dg_ref,
    stats_ref,
    *refs,
):
    out_refs, refs = refs[:pair], refs[pair:]
    gwo_refs, (dy_ref, dz_ref, ggain_ref, acc) = refs[:-4], refs[-4:]
    width = y_ref.shape[1]
    tokens = cot_ref.shape[0] // (chips * pair)
    part = wo_ref.shape[0] // (chips * pair)
    acc[...] = jnp.zeros_like(acc)
    ggain_ref[...] = jnp.zeros_like(ggain_ref)
    gain = gain_ref[...]
    chip, core = spot(pair)

    def device(k, other):
        return lax.rem(chip + k, chips) * pair + (1 - core if other else core)

    def step(k, _):
        for other in range(pair):
            rows = columns_of(device(k, other), tokens)
            st = jnp.concatenate([stats_ref[:, rows], jnp.zeros((6, tokens), F32)], axis=0).T
            r = lax.rsqrt(st[:, 0:1] / inner + EPS)
            y = y_ref[rows, :].astype(F32)
            z = proj_ref[rows, :width].astype(F32)
            sig = jax.nn.sigmoid(z)
            sz = z * sig
            u = y * sz
            dg = dg_ref[rows, :]
            ur = u * r
            gated = (ur * gain).astype(BF)
            du = r * (gain * dg) - u * (r * r * r * (st[:, 1:2] / inner))
            ggain_ref[...] += jnp.sum(dg * ur, axis=0, keepdims=True)
            dy_ref[rows, :] = (du * sz).astype(BF)
            dz_ref[rows, :] = (du * y * (sig * (1.0 + z * (1.0 - sig)))).astype(BF)
            out_refs[other][k, :tokens] = dot(gated, wo_ref[...], 1, 1).astype(BF)
            acc[...] += dot(cot_ref[rows, :], gated, 0, 0)
        return 0

    lax.fori_loop(0, chips, step, 0, unroll=2)
    for k in range(chips):
        for other in range(pair):
            piece = acc[columns_of(device(k, other), part), :].astype(BF)
            if gwo_refs:
                gwo_refs[other][k] = piece
                continue
            rows = out_refs[other].shape[1] - tokens
            for j in range(part // rows):
                lanes = slice(j * width, (j + 1) * width)
                out_refs[other][k, tokens:, lanes] = piece[j * rows : (j + 1) * rows]


def backward_kernel(
    heads,
    chips,
    pair,
    shards,
    proj_ref,
    core_ref,
    open_ref,
    dy_ref,
    dz_ref,
    cw_ref,
    cb_ref,
    hp_ref,
    *refs,
):
    w_refs, refs = refs[:shards], refs[shards:]
    dn_refs, refs = refs[:pair], refs[pair:]
    dproj_ref, gcw_ref, gcb_ref, ghp_ref, dstate, ahead = refs
    shard = w_refs[0].shape[1]
    tokens = proj_ref.shape[0] // (chips * pair)
    per = tokens // GROUP
    at = [peer_from(lax.axis_index("fsdp"), k, shards) for k in range(shards)]
    chip, core = spot(pair)
    width = heads * HEAD_DIM
    chans = width + 2 * STATE
    blocks = proj_ref.shape[0] // GROUP
    dstate[...] = jnp.zeros_like(dstate)
    ahead[...] = jnp.zeros_like(ahead)
    gcw_ref[...] = jnp.zeros_like(gcw_ref)
    gcb_ref[...] = jnp.zeros_like(gcb_ref)
    ghp_ref[...] = jnp.zeros_like(ghp_ref)
    fold = (
        lax.broadcasted_iota(jnp.int32, (width, LANES), 0) // HEAD_DIM
        == lax.broadcasted_iota(jnp.int32, (width, LANES), 1)
    ).astype(F32).astype(BF)

    def step(n, _):
        i = blocks - 1 - n
        rows = pl.ds(pl.multiple_of(i * GROUP, GROUP), GROUP)
        v = proj_ref[rows, width : width + chans].astype(F32)
        taps = conv_taps(v, halo_of(proj_ref, i, width, width + chans))
        cw = cw_ref[...]
        pre = conv_pre(taps, cw, cb_ref[...])
        sig = jax.nn.sigmoid(pre)
        act = pre * sig
        xs = act[:, :width]
        bs = act[:, width : width + STATE].astype(BF)
        cs = act[:, width + STATE :].astype(BF)
        shifted = widen(proj_ref[rows, width + chans :].astype(F32)) + hp_ref[0:1]
        dt = softplus(shifted)
        neg = -jnp.exp(hp_ref[1:2])
        rate = neg * dt
        run = pick_sums(tri(True).astype(F32).astype(BF), rate, 1, 0)
        run_t = run.T
        last = run[GROUP - 1 : GROUP]
        dt_x = spread(dt, heads)
        xdt = (xs * dt_x).astype(BF)
        scores = dot(cs, bs, 1, 1)
        causal = tri(True)
        dyb = dy_ref[rows, :]
        dy = dyb.astype(F32)
        dscores = jnp.zeros((GROUP, GROUP), F32)
        parts = []
        for h in range(heads):
            cols = slice(h * HEAD_DIM, (h + 1) * HEAD_DIM)
            gap = run[:, h : h + 1] - run_t[h : h + 1, :]
            decay = jnp.exp(jnp.where(causal, gap, -1e30))
            mixed = (scores * decay).astype(BF)
            parts.append(dot(mixed, dyb[:, cols], 0, 0))
            dscores = dscores + dot(dyb[:, cols], xdt[:, cols], 1, 1) * decay
        dscores = dscores.astype(BF)
        memory = open_ref[i]
        mem_b = memory.astype(BF)
        ds = dstate[...]
        ds_b = ds.astype(BF)
        edy = (spread(jnp.exp(run), heads) * dy).astype(BF)
        dec = spread(jnp.exp(last - run), heads)
        xdt_f = xdt.astype(F32)
        inflow = dec * dot(bs, ds_b, 1, 0)
        dxdt = jnp.concatenate(parts, axis=1) + inflow
        dc = dot(dscores, bs, 1, 0) + dot(edy, mem_b, 1, 1)
        db = dot(dscores, cs, 0, 0) + dot((xdt_f * dec).astype(BF), ds_b, 1, 1)
        carried = spread(jnp.exp(last), heads)
        dstate[...] = dot(cs, edy, 0, 0) + carried * ds
        dx = dt_x * dxdt + spread(hp_ref[2:3], heads) * dy
        tops = jnp.concatenate(
            [
                jnp.sum(xdt_f * inflow, axis=0, keepdims=True)
                + carried * jnp.sum(ds * memory, axis=0, keepdims=True),
                jnp.sum(dy * xs, axis=0, keepdims=True),
                jnp.zeros((6, width), F32),
            ],
            axis=0,
        )
        folded = pick_sums(
            fold,
            jnp.concatenate([xs * dxdt, dy * core_ref[rows, :] - xdt_f * dxdt, tops], axis=0),
            0,
            1,
            first=False,
        )
        dend = folded[2 * GROUP : 2 * GROUP + 1]
        drate = pick_sums(tri(False).astype(F32).astype(BF), folded[GROUP : 2 * GROUP], 1, 0) + dend
        ddt = folded[:GROUP] + neg * drate
        ddtr = ddt * jax.nn.sigmoid(shifted)
        ghp_ref[0:1] += jnp.sum(ddtr, axis=0, keepdims=True)
        ghp_ref[1:2] += jnp.sum(drate * rate, axis=0, keepdims=True)
        ghp_ref[2:3] += folded[2 * GROUP + 1 : 2 * GROUP + 2]
        dact = jnp.concatenate([dx, db, dc], axis=1)
        dpre = dact * (sig * (1.0 + pre * (1.0 - sig)))
        gcb_ref[...] += jnp.sum(dpre, axis=0, keepdims=True)
        for k in range(CONV_W):
            gcw_ref[k : k + 1] += jnp.sum(dpre * taps[k], axis=0, keepdims=True)
        ext = jnp.concatenate([dpre, ahead[...]], axis=0)
        ahead[...] = dpre[:HALO]
        dv = cw[CONV_W - 1 :] * dpre
        for k in range(CONV_W - 1):
            moved = pltpu.roll(ext, ext.shape[0] - (CONV_W - 1 - k), 0)[:GROUP]
            dv = dv + cw[k : k + 1] * moved
        few = dproj_ref.shape[1] - width - chans
        dproj = jnp.concatenate(
            [dz_ref[rows, :], dv.astype(BF), ddtr[:, :few].astype(BF)], axis=1
        )
        dproj_ref[rows, :] = dproj
        owner = i // per
        k = lax.rem(owner // pair - chip + chips, chips)
        inside = pl.ds(pl.multiple_of((i % per) * GROUP, GROUP), GROUP)
        dn = [dot(dproj, w[...], 1, 0).astype(BF) for w in w_refs]
        for other in range(pair):

            @pl.when((owner % pair != core) == bool(other))
            def _():
                for j in range(shards):
                    dn_refs[other][k, inside, columns_of(at[j], shard)] = dn[j]

        return 0

    lax.fori_loop(0, blocks, step, 0, unroll=2)


def columns_kernel(heads, shards, dproj_ref, normed_ref, *refs):
    w_refs, refs = refs[:shards], refs[shards:]
    gcw_ref, gcb_ref, ghp_ref, ggain_ref, refs = *refs[:4], refs[4:]
    g_refs, (gnorm_ref, slots_ref, common_ref) = refs[:shards], refs[shards:]
    width = ggain_ref.shape[1]
    lanes = min(width, LANES)
    packed = ghp_ref[0:1]
    for n in range(1, 3):
        packed = packed + pltpu.roll(ghp_ref[n : n + 1], n * heads, 1)
    packed = packed[:, :lanes]
    if lanes < width:
        packed = jnp.concatenate([packed, jnp.zeros((1, width - lanes), F32)], axis=1)
    slots_ref[...] = jnp.zeros_like(slots_ref)
    slot = jnp.concatenate(
        [
            gcw_ref[:, :width],
            gcb_ref[:, :width],
            ggain_ref[...],
            packed,
            jnp.zeros((1, width), F32),
        ],
        axis=0,
    )
    for j in range(width // lanes):
        slots_ref[lax.axis_index("seq"), j] = slot[:, j * lanes : (j + 1) * lanes]
    for j in range(2 * STATE // LANES):
        at = slice(width + j * LANES, width + (j + 1) * LANES)
        common_ref[j] = jnp.concatenate(
            [gcw_ref[:, at], gcb_ref[:, at], jnp.zeros((3, LANES), F32)], axis=0
        )
    shard = w_refs[0].shape[1]
    for k in range(shards):
        at = columns_of(peer_to(lax.axis_index("fsdp"), k, shards), shard)
        g = dot(dproj_ref[...], normed_ref[:, at], 0, 0)
        g_refs[k][...] = g.astype(BF)
        source = peer_index(k, shards)
        gnorm_ref[0:1, at] = jnp.sum(g * w_refs[source][...].astype(F32), axis=0, keepdims=True)


def chosen(index, start, size):
    row = lax.broadcasted_iota(jnp.int32, (size, index.shape[1]), 0) + start
    return (row == index).astype(F32).astype(BF)


def table_row(table_ref):
    return table_ref[pl.ds(lax.axis_index("seq"), 1), :]


def pick_kernel(table_ref, w_ref, *out_refs):
    index, start = table_row(table_ref), 0
    for out_ref in out_refs:
        items = index[:, start : start + out_ref.shape[0]]
        out_ref[...] = dot(chosen(items, 0, w_ref.shape[0]), w_ref[...], 0, 0).astype(BF)
        start += out_ref.shape[0]


def place_kernel(split, kinds, table_ref, w_ref, *refs):
    arrived, out_refs = refs[:-2], refs[-2:]
    index = table_row(table_ref)
    for kind, out_ref in enumerate(out_refs):
        rows = slice(kind * split, kind * split + out_ref.shape[0])
        start = w_ref.shape[0]
        out = dot(chosen(index[:, rows], 0, start), w_ref[...], 0, 0)
        for shared, piece in zip(kinds, arrived):
            if shared is None or shared == bool(kind):
                out = out + dot(chosen(index[:, rows], start, piece.shape[0]), piece[...], 0, 0)
            start += piece.shape[0]
        out_ref[...] = out.astype(BF)


def back_kernel(kinds, table_ref, g_ref, common_ref, pool_ref, *out_refs):
    split = pool_ref.shape[0] - common_ref.shape[0]
    pool_ref[:split] = g_ref[:split]
    pool_ref[split:] = common_ref[...]
    index, start = table_row(table_ref), 0
    for shared, out_ref in zip(kinds, out_refs):
        items = index[:, start : start + out_ref.shape[0]]
        if shared is None:
            out = dot(chosen(items, 0, pool_ref.shape[0]), pool_ref[...], 0, 0)
        elif shared:
            out = dot(chosen(items, split, common_ref.shape[0]), common_ref[...], 0, 0)
        else:
            out = dot(chosen(items, 0, split), g_ref[:split], 0, 0)
        out_ref[...] = out.astype(BF)
        start += out_ref.shape[0]


def home_kernel(table_ref, *refs):
    pieces, out_ref = refs[:-1], refs[-1]
    index, start, out = table_row(table_ref), 0, None
    for piece in pieces:
        items = index[:, start : start + piece.shape[0]]
        part = dot(chosen(items, 0, out_ref.shape[0]), piece[...], 1, 0)
        out = part if out is None else out + part
        start += piece.shape[0]
    out_ref[...] = out


def hold_kernel(tokens, keep_ref, got_ref, own_ref, *out_refs):
    rows = keep_ref.shape[1]
    for k in range(keep_ref.shape[0]):
        total = keep_ref[k, :tokens].astype(F32) + got_ref[k, :tokens].astype(F32)
        if k == 0:
            own_ref[:tokens] = total
        else:
            out_refs[k - 1][:tokens] = total.astype(BF)
        if rows > tokens:
            extra = rows - tokens
            for n, ref in enumerate((keep_ref, got_ref)):
                at = slice(tokens + n * extra, tokens + (n + 1) * extra)
                if k == 0:
                    own_ref[at] = ref[k, tokens:].astype(F32)
                else:
                    out_refs[k - 1][at] = ref[k, tokens:]


def peer_index(k, count):
    return k if count & (count - 1) == 0 else (count - k) % count


def call(kernel, outs, scratch, *args):
    whole = pl.BlockSpec(memory_space=pltpu.VMEM)
    return pl.pallas_call(
        kernel,
        out_shape=[jax.ShapeDtypeStruct(shape, kind) for shape, kind in outs],
        in_specs=[whole] * len(args),
        out_specs=[whole] * len(outs),
        scratch_shapes=[pltpu.VMEM(shape, kind) for shape, kind in scratch],
    )(*args)


def per_device(
    fsdp,
    seq,
    block_input,
    norm_gain,
    w_in,
    conv_w,
    conv_b,
    dt_bias,
    a_log,
    skip_gain,
    gate_gain,
    w_out,
    out_cotangent,
):
    links = Links(fsdp, seq)
    residual = block_input[0]
    grad_out = out_cotangent[0]
    tokens, depth = residual.shape
    length = tokens * seq
    heads_all = dt_bias.shape[0]
    inner = gate_gain.shape[0]
    heads = heads_all // seq
    width = inner // seq
    chans = width + 2 * STATE
    sizes = (seq, w_in.shape[1] * seq, inner, STATE, heads_all)
    routes = Routes(*sizes)
    homes = Routes(*sizes, merged=True)
    me = links.s
    shared = routes.shared

    mean = jnp.mean(residual * residual, axis=-1, keepdims=True)
    scale = lax.rsqrt(mean + EPS)
    normed_half = (residual * scale * norm_gain).astype(BF)

    w_cols = w_in.T
    rows_here = w_in.shape[0]
    picked = call(
        pick_kernel,
        [((size, rows_here), BF) for size in routes.sizes],
        [],
        jnp.asarray(routes.send),
        w_cols,
    )
    arrived = []
    for r, group in enumerate(routes.rounds):
        arrived.append(lax.ppermute(picked[r], "seq", [(p[0], p[1]) for p in group]))
    mine, common = call(
        functools.partial(place_kernel, 2 * width, routes.kinds),
        [((2 * width, rows_here), BF), ((shared, rows_here), BF)],
        [],
        jnp.asarray(routes.take),
        w_cols,
        *arrived,
    )
    if links.pair == 2:
        common = common + lax.ppermute(
            common, "seq", [(i, i - 1) for i in range(1, seq, 2)]
        )
    head_row = jnp.arange(ceil_to(heads, 16), dtype=jnp.int32)
    head_row = jnp.where(head_row < heads, 2 * STATE + me * heads + head_row, -1)
    head_pick = one_hot(head_row, shared)
    w_mine = jnp.concatenate(
        [mine, common[: 2 * STATE], dot(head_pick, common, 1, 0).astype(BF)], axis=0
    )
    normed = links.gather_seq(normed_half)
    w_all = links.gather_fsdp(w_mine)

    wo_half = w_out.reshape(-1, width, w_out.shape[1]).transpose(0, 2, 1)
    wo_rows = jnp.zeros((fsdp,) + wo_half.shape, BF)
    for k, piece in enumerate(links.gather_fsdp(wo_half)):
        wo_rows = lax.dynamic_update_index_in_dim(wo_rows, piece, peer_from(links.f, k, fsdp), 0)
    wo_rows = wo_rows.reshape((links.chips, links.pair) + wo_half.shape[1:])
    order = [links.chip_at(k) for k in range(links.chips)]

    def parity(core):
        picks = [lax.dynamic_slice(wo_rows, (c, core, 0, 0), (1, 1) + wo_half.shape[1:]) for c in order]
        return jnp.concatenate(picks, axis=0)[:, 0]

    wo = links.exchange_seq(parity(links.core), parity(1 - links.core))
    cot_half = grad_out.astype(BF)
    cot = links.gather_seq(cot_half)

    def local(vector, size, start):
        return lax.dynamic_slice_in_dim(vector, start, size, vector.ndim - 1)

    cw = jnp.concatenate([local(conv_w[:, :inner], width, me * width), conv_w[:, inner:]], axis=1)
    cb = jnp.concatenate([local(conv_b[:inner], width, me * width), conv_b[inner:]])[None]
    per_head = jnp.stack([local(p, heads, me * heads) for p in (dt_bias, a_log, skip_gain)])
    hp = jnp.pad(per_head, ((0, 5), (0, LANES - heads)))
    gain = local(gate_gain, width, me * width)[None]
    narrow = ceil_to(heads, 16)
    cols = 2 * width + 2 * STATE + narrow
    blocks = length // GROUP

    chips, pair = links.chips, links.pair
    normed_all, proj, y, core, opened = call(
        functools.partial(forward_kernel, heads, chips, pair, fsdp),
        [
            ((length, depth), BF),
            ((length, cols), BF),
            ((length, width), BF),
            ((length, width), F32),
            ((blocks, STATE, width), F32),
        ],
        [((STATE, width), F32)],
        *normed,
        *w_all,
        cw,
        cb,
        hp,
    )
    cot_all, wo_all, dgated, stats = call(
        functools.partial(stats_kernel, chips, pair),
        [((length, depth), BF), ((depth, width), BF), ((length, width), F32), ((2, length), F32)],
        [],
        *cot,
        *wo,
        y,
        proj,
        gain,
    )
    stats = links.sum_seq(stats)
    halves = [((chips, tokens, depth), BF)] * pair
    part = depth // seq
    extra = part * width // depth
    together = pair == 2 and extra % 16 == 0 and width % LANES == 0
    out_halves = [((chips, tokens + extra, depth), BF)] * pair if together else halves
    quarters = [] if together else [((chips, part, width), BF)] * pair
    gate_outs = call(
        functools.partial(gate_kernel, float(inner), chips, pair),
        out_halves
        + quarters
        + [((length, width), BF), ((length, width), BF), ((1, width), F32)],
        [((depth, width), F32)],
        cot_all,
        wo_all,
        y,
        proj,
        gain,
        dgated,
        stats,
    )
    out_halves, gwo_halves = gate_outs[:pair], gate_outs[pair:-3]
    dy, dz, ggain = gate_outs[-3:]
    back_outs = call(
        functools.partial(backward_kernel, heads, chips, pair, fsdp),
        halves
        + [((length, cols), BF), ((CONV_W, chans), F32), ((1, chans), F32), ((8, LANES), F32)],
        [((STATE, width), F32), ((HALO, chans), F32)],
        proj,
        core,
        opened,
        dy,
        dz,
        cw,
        cb,
        hp,
        *w_all,
    )
    dn_halves = back_outs[:pair]
    dproj, gcw, gcb, ghp = back_outs[pair:]
    shard = depth // fsdp
    lanes = min(width, LANES)
    *g_cols, g_norm, slots, g_shared = call(
        functools.partial(columns_kernel, heads, fsdp),
        [((cols, shard), BF)] * fsdp
        + [
            ((1, depth), F32),
            ((seq, width // lanes, 8, lanes), F32),
            ((2 * STATE // LANES, 8, LANES), F32),
        ],
        [],
        dproj,
        normed_all,
        *w_all,
        gcw,
        gcb,
        ghp,
        ggain,
    )

    out_sum, arrived = links.scatter_seq(out_halves[0], out_halves[-1], tokens)
    block_out = residual + out_sum
    if together:
        gwo = []
        for piece in arrived:
            both = piece[tokens:].astype(BF).reshape(2, extra, part // extra, width)
            both = both.transpose(0, 2, 1, 3).reshape(2, part, width)
            gwo.append(jnp.where(links.core == 0, both, both[::-1]))
    else:
        gwo = links.exchange_seq(gwo_halves[0], gwo_halves[-1])
    gwo_rows = jnp.zeros((chips,) + gwo[0].shape, BF)
    for k, piece in enumerate(gwo):
        gwo_rows = lax.dynamic_update_index_in_dim(gwo_rows, piece, links.chip_at(-k), 0)
    gwo_rows = gwo_rows.reshape((fsdp, seq // fsdp, depth // seq, width))
    to = [
        lax.dynamic_index_in_dim(gwo_rows, peer_to(links.f, k, fsdp), 0, keepdims=False)
        for k in range(fsdp)
    ]
    owned_w_out = links.scatter_fsdp(to).transpose(0, 2, 1).reshape(w_out.shape)

    g_mine = links.scatter_fsdp(g_cols)
    dnormed, _ = links.scatter_seq(dn_halves[0], dn_halves[-1], tokens)
    dscaled = dnormed * norm_gain
    du_norm = scale * dscaled - residual * (
        scale * scale * scale * jnp.mean(residual * dscaled, axis=-1, keepdims=True)
    )
    grad_in = grad_out + du_norm

    g_half = g_mine.astype(BF)
    g_heads = dot(head_pick, g_half[2 * width + 2 * STATE :], 0, 0)[2 * STATE :]
    g_common = jnp.concatenate([g_half[2 * width : 2 * width + 2 * STATE], g_heads.astype(BF)])
    if links.pair == 2:
        other = lax.ppermute(g_common, "seq", [(i, i + 1) for i in range(0, seq, 2)])
        g_common = (g_common.astype(F32) + other.astype(F32)).astype(BF)
    g_pool, *sent = call(
        functools.partial(back_kernel, homes.kinds),
        [((homes.rows, rows_here), BF)] + [((size, rows_here), BF) for size in homes.sizes],
        [],
        jnp.asarray(homes.back),
        g_half,
        g_common,
    )
    homed = []
    for r, group in enumerate(homes.rounds):
        homed.append(lax.ppermute(sent[r], "seq", [(p[1], p[0]) for p in group]))
    (owned_w_in,) = call(
        home_kernel, [(w_cols.shape, F32)], [], jnp.asarray(homes.home), g_pool, *homed
    )
    owned_w_in = owned_w_in.T

    pieces, _ = lax.optimization_barrier(([slots, g_shared, g_norm], tuple(g_cols)))
    packed = jnp.concatenate([p.reshape(-1, LANES) for p in pieces], axis=0)
    packed = links.sum_fsdp(links.sum_seq(packed))
    first = slots.size // LANES
    slots = packed[:first].reshape(slots.shape)
    second = first + g_shared.size // LANES
    g_shared = packed[first:second].reshape(g_shared.shape)
    g_norm = packed[second:].reshape(-1) / norm_gain
    slots = slots.transpose(0, 2, 1, 3).reshape(seq, 8, width)
    g_shared = g_shared.transpose(1, 0, 2).reshape(8, 2 * STATE)
    g_conv_w = jnp.concatenate(
        [slots[:, :CONV_W].transpose(1, 0, 2).reshape(CONV_W, inner), g_shared[:CONV_W]], axis=1
    )
    g_conv_b = jnp.concatenate([slots[:, CONV_W].reshape(inner), g_shared[CONV_W]])
    g_gain = slots[:, CONV_W + 1].reshape(inner)
    g_head = [slots[:, CONV_W + 2, n * heads : (n + 1) * heads].reshape(-1) for n in range(3)]
    return (
        block_out[None],
        grad_in[None],
        g_norm,
        owned_w_in,
        g_conv_w,
        g_conv_b,
        *g_head,
        g_gain,
        owned_w_out,
    )


def solution(mesh):
    weights = P("fsdp", "seq")
    acts = P("fsdp", "seq", None)
    fsdp, seq = mesh.shape["fsdp"], mesh.shape["seq"]

    def body(*args):
        return per_device(fsdp, seq, *args)

    return jax.shard_map(
        body,
        mesh=mesh,
        in_specs=(acts, P(), weights, P(), P(), P(), P(), P(), P(), weights, acts),
        out_specs=(acts, acts, P(), weights, P(), P(), P(), P(), P(), P(), weights),
        check_vma=False,
    )
```
